32 devices in a mesh: cluster: 16 (over z, x, core), blk: 2 (over y).
Axes of the slice: x: 2, y: 2, z: 4, core: 2. Of those that a mesh axis runs over, the one named last changes fastest.
Arguments:
- coeff: bfloat16 [512, 8, 2048], P('cluster', None, 'blk'), may hold values from -0.375 to 0.375
- intersection: int32 [16, 32], replicated, may hold values from 0 to 511, as said below
- basis_vals: bfloat16 [8192, 256], P(('cluster', 'blk')), may hold values from -6 to 6
- coulomb: bfloat16 [8192, 7, 256], P(('cluster', 'blk')), may hold values from -0.125 to 0.125
- reach: int32 [32], P(('cluster', 'blk')), may hold values from 0 to 3, as said below
Outputs:
- exchange_out: bfloat16 [8192, 2048], P(('cluster', 'blk'))
The draws below stay inside these ranges and needn't reach their ends.
Inputs may be any that keep to these rules, and one draw needn't show every extreme that they name: `intersection`: each row lists 32 distinct atoms; atom a is owned by cluster a // 32; at most 4 atoms of one row have the same owner, and each row c holds exactly 4 atoms owned by cluster c. `reach`: some block reaches 3 and some block reaches 0.
All inputs are finite; a program needn't handle non-finite values.
Results may differ from the reference program's by a relative error of at most 0.0059.
Values may be sent and summed in bfloat16 or wider, within the bound.
No kernel may reach another device: no remote copies, remote signals or barrier semaphores. Data moves between devices by JAX's collectives and lax.ppermute only.
A program may use at most 64 MiB of HBM per device.

```python
import jax
import jax.numpy as jnp
from jax import lax

NORB = 2048
NAO = 8
NEED = 32
HALF_STOPS = 3
PTS_DEV = 256
ATOM_CL = 32
STOPS = 7
SLOT = 4
NCLUST = 16
BLOCKS = 32
NPTS = 8192
ATOMS = 512
N_BLK = 2


def draw_intersection(key, part):
    total_slots = NCLUST * SLOT

    def one_row(cluster_id):
        row_key = jax.random.fold_in(jax.random.fold_in(key, 4101), cluster_id)
        shuffled = jax.random.permutation(jax.random.fold_in(row_key, 1), total_slots)
        owners = shuffled // SLOT
        priority = jnp.where(owners == cluster_id, 0, 1) * total_slots + jnp.arange(total_slots, dtype=jnp.int32)
        ranking = jnp.argsort(priority)
        chosen = shuffled[ranking][:NEED]
        chosen = chosen[jax.random.permutation(jax.random.fold_in(row_key, 2), NEED)]
        chosen_owner = chosen // SLOT
        slot_pos = chosen % SLOT
        offsets = jax.random.randint(jax.random.fold_in(row_key, 3), (NCLUST,), 0, ATOM_CL)
        return chosen_owner * ATOM_CL + (slot_pos + offsets[chosen_owner]) % ATOM_CL
    rows = jax.vmap(one_row)(jnp.arange(NCLUST, dtype=jnp.int32))
    return rows.astype(jnp.int32)


def draw_reach(key, part):
    base_key = jax.random.fold_in(key, 7303)
    ranges = jax.random.randint(jax.random.fold_in(base_key, 1), (BLOCKS,), 0, HALF_STOPS + 1)
    shuffled = jax.random.permutation(jax.random.fold_in(base_key, 2), BLOCKS)
    ranges = ranges.at[shuffled[0]].set(HALF_STOPS)
    ranges = ranges.at[shuffled[1]].set(0)
    return ranges.astype(jnp.int32)


def block_levels(own_key, dims, split, smallest, high):
    level = 1.0
    for axis_at, parts in split:
        draws = jax.random.uniform(jax.random.fold_in(jax.random.fold_in(own_key, 6), axis_at), (parts,), jnp.float32, smallest / len(split), high / len(split))
        level = level * jnp.repeat(jnp.exp(draws), dims[axis_at] // parts).reshape((-1,) + (1,) * (len(dims) - 1 - axis_at))
    return level


def scatter_about(own_key, shape, deviation, bound, cuts=(), held_as=jnp.bfloat16):
    array = jax.random.normal(own_key, shape, jnp.float32) * deviation
    if len(cuts) > 0:
        array = block_levels(own_key, shape, cuts, -0.22, 0.18) * array
    return jnp.clip(array, min=-bound, max=bound).astype(held_as)


def setup_inputs(seed: int = 0) -> dict:
    keys = jax.random.split(jax.random.key(seed), 6)
    return {
        "coeff": scatter_about(keys[0], (ATOMS, NAO, NORB), (NEED * NAO) ** -0.5, 0.375, ((0, 16), (2, 2))),
        "intersection": draw_intersection(jax.random.fold_in(keys[5], 71), 0),
        "basis_vals": scatter_about(keys[2], (NPTS, NEED * NAO), 1.0, 6.0, ((0, 32),)),
        "coulomb": scatter_about(keys[3], (NPTS, STOPS, PTS_DEV), (STOPS * PTS_DEV) ** -0.5, 0.125, ((0, 32),)),
        "reach": draw_reach(jax.random.fold_in(keys[5], 71), 0),
    }


def reference(coeff, intersection, basis_vals, coulomb, reach):
    num_clusters = intersection.shape[0]
    half_stops = (coulomb.shape[1] - 1) // 2
    norm_factor = NORB ** -0.5

    def orbit(cluster_id):
        coeff_rows = coeff[intersection[cluster_id]].reshape(NEED * NAO, NORB)
        basis_block = lax.dynamic_slice_in_dim(basis_vals, cluster_id * (N_BLK * PTS_DEV), N_BLK * PTS_DEV, 0)
        return jnp.dot(basis_block, coeff_rows, preferred_element_type=jnp.float32).astype(jnp.bfloat16)

    orbitals = lax.map(orbit, jnp.arange(num_clusters, dtype=jnp.int32))
    orbitals = orbitals.reshape(num_clusters, N_BLK, PTS_DEV, NORB)
    coul_blocks = coulomb.reshape(num_clusters, N_BLK, PTS_DEV, coulomb.shape[1], PTS_DEV)
    reach_blocks = reach.reshape(num_clusters, N_BLK)

    def one_block(block_id):
        cluster_id = block_id // N_BLK
        blk_id = block_id % N_BLK
        local_vals = orbitals[cluster_id, blk_id]
        accumulated = jnp.zeros((PTS_DEV, NORB), jnp.float32)
        for offset in range(-half_stops, half_stops + 1):
            source_id = (blk_id + offset) % N_BLK
            source = orbitals[cluster_id, source_id]
            density = lax.dot_general(local_vals, source, (((1,), (1,)), ((), ())), preferred_element_type=jnp.float32) * norm_factor
            within = abs(offset) <= reach_blocks[cluster_id, blk_id]
            masked_tile = jnp.where(within, density * coul_blocks[cluster_id, blk_id, :, offset + half_stops, :].astype(jnp.float32), jnp.float32(0.0)).astype(jnp.bfloat16)
            accumulated = accumulated + jnp.dot(masked_tile, source, preferred_element_type=jnp.float32)
        return accumulated.astype(jnp.bfloat16)

    result = lax.map(one_block, jnp.arange(num_clusters * N_BLK, dtype=jnp.int32))
    return result.reshape(NPTS, NORB)
```

```python
import jax
import jax.numpy as jnp
from jax import lax
from jax.experimental import pallas as pl
from jax.experimental.pallas import tpu as pltpu
from jax.sharding import PartitionSpec as P


def passed_along(value, axis, steps):
    count = lax.axis_size(axis)
    pairs = [(source, (source + steps) % count) for source in range(count)]
    return lax.ppermute(value, axis, pairs)


def split_high_low(value):
    high = value.astype(jnp.bfloat16)
    low = (value - high.astype(jnp.float32)).astype(jnp.bfloat16)
    return high, low


def dot_nn(a, b):
    return lax.dot_general(a, b, (((1,), (0,)), ((), ())), preferred_element_type=jnp.float32)


def dot_nt(a, b):
    return lax.dot_general(a, b, (((1,), (1,)), ((), ())), preferred_element_type=jnp.float32)


def exchange_kernel(num_sources, num_parts, has_gram, *refs):
    offsets = refs[0]
    basis_refs = refs[1 : 1 + num_sources]
    factor_refs = refs[1 + num_sources : 1 + 2 * num_sources]
    rest = refs[1 + 2 * num_sources :]
    if has_gram:
        gram = rest[0][...]
        rest = rest[1:]
        fresh = range(1, num_parts)
    else:
        gram = None
        fresh = range(num_parts)
    part_refs = rest[:num_parts]
    out_ref = rest[num_parts]
    for part in fresh:
        term = dot_nt(part_refs[part][...], part_refs[part][...])
        gram = term if gram is None else gram + term
    gram_high, gram_low = split_high_low(gram)
    own = basis_refs[0][...]
    projected = dot_nn(own, gram_high) + dot_nn(own, gram_low)
    proj_high, proj_low = split_high_low(projected)
    mixed = None
    for source in range(num_sources):
        basis = basis_refs[source][...]
        density = dot_nt(proj_high, basis) + dot_nt(proj_low, basis)
        tile = (density * factor_refs[source][...]).astype(jnp.bfloat16)
        term = dot_nn(tile, basis)
        mixed = term if mixed is None else mixed + term
    mixed_high, mixed_low = split_high_low(mixed)
    for part in range(num_parts):
        values = part_refs[part][...]
        width = values.shape[1]
        result = dot_nn(mixed_high, values) + dot_nn(mixed_low, values)
        start = pl.multiple_of(offsets[part] * width, width)
        out_ref[:, pl.ds(start, width)] = result.astype(out_ref.dtype)


def on_device(coeff, intersection, basis_vals, coulomb, reach):
    num_clusters = lax.axis_size("cluster")
    num_blocks = lax.axis_size("blk")
    my_cluster = lax.axis_index("cluster")
    my_block = lax.axis_index("blk")
    atom_count, num_funcs, my_columns = coeff.shape
    list_len = intersection.shape[1]
    capacity = 2 * list_len // num_clusters
    half_stops = (coulomb.shape[1] - 1) // 2
    points = basis_vals.shape[0]
    norm_factor = (my_columns * num_blocks) ** (-0.5)

    local_atom = intersection - my_cluster * atom_count
    mine = jnp.logical_and(local_atom >= 0, local_atom < atom_count)
    earlier = jnp.arange(list_len)[:, None] < jnp.arange(list_len)[None, :]
    rank = jnp.dot(mine.astype(jnp.bfloat16), earlier.astype(jnp.bfloat16), preferred_element_type=jnp.float32)
    rank = rank.astype(jnp.int32)
    matches = jnp.logical_and(mine[:, None, :], rank[:, None, :] == jnp.arange(capacity)[None, :, None])
    source_rows = jnp.sum(jnp.where(matches, local_atom[:, None, :], 0), axis=2)
    outgoing = coeff.at[source_rows.reshape(-1)].get(mode="promise_in_bounds")
    outgoing = outgoing.reshape(num_clusters, capacity, num_funcs, my_columns)
    incoming = lax.all_to_all(outgoing, "cluster", split_axis=0, concat_axis=0, tiled=True)

    my_row = lax.dynamic_index_in_dim(intersection, my_cluster, 0, keepdims=False)
    my_owners = my_row // atom_count
    same = jnp.logical_and(my_owners[:, None] == my_owners[None, :], earlier.T)
    my_ranks = jnp.sum(same.astype(jnp.int32), axis=1)
    positions = my_owners * capacity + my_ranks
    needed = incoming.reshape(num_clusters * capacity, num_funcs, my_columns)
    needed = needed.at[positions].get(mode="promise_in_bounds")
    needed = needed.reshape(list_len * num_funcs, my_columns)

    by_step = {}
    for offset in range(-half_stops, half_stops + 1):
        by_step.setdefault(offset % num_blocks, []).append(offset)
    steps = sorted(by_step)
    my_reach = reach[0]
    sources = []
    factors = []
    for step in steps:
        sources.append(basis_vals if step == 0 else passed_along(basis_vals, "blk", -step))
        total = jnp.zeros((points, points), jnp.float32)
        for offset in by_step[step]:
            tile = coulomb[:, offset + half_stops, :].astype(jnp.float32)
            total = total + jnp.where(abs(offset) <= my_reach, tile, jnp.float32(0.0))
        factors.append(total * norm_factor)

    if num_blocks == 2:
        other = passed_along(needed, "blk", 1)
        gram = [dot_nt(needed, needed)]
        parts = [needed, other]
        offsets = jnp.stack([my_block, 1 - my_block])
    else:
        gram = []
        parts = [lax.all_gather(needed, "blk", axis=1, tiled=True)]
        offsets = jnp.zeros((1,), jnp.int32)

    vmem = pl.BlockSpec(memory_space=pltpu.VMEM)
    operands = [offsets, *sources, *factors, *gram, *parts]

    def kernel(*refs):
        exchange_kernel(len(sources), len(parts), bool(gram), *refs)

    return pl.pallas_call(
        kernel,
        out_shape=jax.ShapeDtypeStruct((points, my_columns * num_blocks), jnp.bfloat16),
        in_specs=[pl.BlockSpec(memory_space=pltpu.SMEM)] + [vmem] * (len(operands) - 1),
        out_specs=vmem,
        name="exchange",
    )(*operands)


def solution(mesh):
    return jax.shard_map(
        on_device,
        mesh=mesh,
        in_specs=(
            P("cluster", None, "blk"),
            P(),
            P(("cluster", "blk"), None),
            P(("cluster", "blk"), None, None),
            P(("cluster", "blk")),
        ),
        out_specs=P(("cluster", "blk"), None),
        check_vma=False,
    )
```

```python
import jax
import jax.numpy as jnp
from jax import lax
from jax.experimental import pallas as pl
from jax.experimental.pallas import tpu as pltpu
from jax.sharding import PartitionSpec as P


VMEM = pl.BlockSpec(memory_space=pltpu.VMEM)
SMEM = pl.BlockSpec(memory_space=pltpu.SMEM)
PARAMS = pltpu.CompilerParams(vmem_limit_bytes=16 * 2**20)


def passed_along(value, axis, steps):
    count = lax.axis_size(axis)
    pairs = [(source, (source + steps) % count) for source in range(count)]
    return lax.ppermute(value, axis, pairs)


def swapped(value, axis, bits):
    count = lax.axis_size(axis)
    return lax.ppermute(value, axis, [(source, source ^ bits) for source in range(count)])


def split_high_low(value):
    high = value.astype(jnp.bfloat16)
    low = (value - high.astype(jnp.float32)).astype(jnp.bfloat16)
    return high, low


def dot_nn(a, b):
    return lax.dot_general(a, b, (((1,), (0,)), ((), ())), preferred_element_type=jnp.float32)


def dot_nt(a, b):
    return lax.dot_general(a, b, (((1,), (1,)), ((), ())), preferred_element_type=jnp.float32)


def stacked(refs):
    values = [ref[...].reshape(-1, ref.shape[-1]) for ref in refs]
    return values[0] if len(values) == 1 else jnp.concatenate(values, axis=0)


def exchange(offsets, sources, factors, gram, parts, width):
    num_sources = len(sources)
    counts = [len(blocks) for blocks in parts]
    points = sources[0].shape[0]

    def kernel(*refs):
        offset_ref = refs[0]
        basis_refs = refs[1 : 1 + num_sources]
        factor_refs = refs[1 + num_sources : 1 + 2 * num_sources]
        rest = list(refs[1 + 2 * num_sources :])
        total = rest.pop(0)[...] if gram is not None else None
        part_values = []
        for count in counts:
            part_values.append(stacked(rest[:count]))
            rest = rest[count:]
        out_ref = rest[0]
        for values in part_values[0 if gram is None else 1 :]:
            term = dot_nt(values, values)
            total = term if total is None else total + term
        gram_high, gram_low = split_high_low(total)
        own = basis_refs[0][...]
        projected = dot_nn(own, gram_high) + dot_nn(own, gram_low)
        proj_high, proj_low = split_high_low(projected)
        mixed = None
        for source in range(num_sources):
            basis = basis_refs[source][...]
            density = dot_nt(proj_high, basis) + dot_nt(proj_low, basis)
            tile = (density * factor_refs[source][...]).astype(jnp.bfloat16)
            term = dot_nn(tile, basis)
            mixed = term if mixed is None else mixed + term
        mixed_high, mixed_low = split_high_low(mixed)
        for part, values in enumerate(part_values):
            columns = values.shape[1]
            result = dot_nn(mixed_high, values) + dot_nn(mixed_low, values)
            start = pl.multiple_of(offset_ref[part] * columns, columns)
            out_ref[:, pl.ds(start, columns)] = result.astype(out_ref.dtype)

    operands = [offsets, *sources, *factors]
    if gram is not None:
        operands.append(gram)
    for blocks in parts:
        operands.extend(blocks)
    return pl.pallas_call(
        kernel,
        out_shape=jax.ShapeDtypeStruct((points, width), jnp.bfloat16),
        in_specs=[SMEM] + [VMEM] * (len(operands) - 1),
        out_specs=VMEM,
        compiler_params=PARAMS,
        name="exchange",
    )(*operands)


def own_gram(blocks):
    rows = sum(block.shape[0] * block.shape[1] for block in blocks)

    def kernel(*refs):
        values = stacked(refs[:-1])
        refs[-1][...] = dot_nt(values, values)

    return pl.pallas_call(
        kernel,
        out_shape=jax.ShapeDtypeStruct((rows, rows), jnp.float32),
        in_specs=[VMEM] * len(blocks),
        out_specs=VMEM,
        compiler_params=PARAMS,
        name="own_gram",
    )(*blocks)


def outgoing_pieces(coeff, intersection, my_cluster, capacity):
    num_clusters, list_len = intersection.shape
    atom_count, num_funcs, columns = coeff.shape
    slots = num_clusters * capacity
    piece_slots = 2 * capacity
    lanes = 128

    def kernel(me_ref, list_ref, coeff_ref, *out_refs):
        me = me_ref[0]
        local = list_ref[...] - me * atom_count
        mine = jnp.logical_and(local >= 0, local < atom_count)
        ks = lax.broadcasted_iota(jnp.int32, (list_len, list_len), 0)
        ls = lax.broadcasted_iota(jnp.int32, (list_len, list_len), 1)
        earlier = jnp.where(ks < ls, 1.0, 0.0).astype(jnp.bfloat16)
        mine_f = jnp.where(mine, 1.0, 0.0)
        rank = dot_nn(mine_f.astype(jnp.bfloat16), earlier)
        local_f = local.astype(jnp.float32)
        lane = lax.broadcasted_iota(jnp.int32, (num_clusters, lanes), 1)
        source = jnp.zeros((num_clusters, lanes), jnp.float32)
        for slot in range(capacity):
            chosen = jnp.where(jnp.logical_and(mine, rank == slot), local_f, 0.0)
            source = jnp.where(lane == slot, jnp.sum(chosen, axis=1, keepdims=True), source)
        rows = slots * num_funcs
        row = lax.broadcasted_iota(jnp.int32, (rows, num_clusters), 0)
        cluster = lax.broadcasted_iota(jnp.int32, (rows, num_clusters), 1)
        pick = jnp.where(cluster == jnp.bitwise_xor(row // (capacity * num_funcs), me), 1.0, 0.0)
        spread = dot_nn(pick.astype(jnp.bfloat16), source.astype(jnp.bfloat16))
        row = lax.broadcasted_iota(jnp.int32, (rows, lanes), 0)
        lane = lax.broadcasted_iota(jnp.int32, (rows, lanes), 1)
        spread = jnp.where(lane == (row // num_funcs) % capacity, spread, 0.0)
        held = atom_count * num_funcs
        atom = dot_nn(spread.astype(jnp.bfloat16), jnp.ones((lanes, held), jnp.bfloat16))
        row = lax.broadcasted_iota(jnp.int32, (rows, held), 0)
        column = lax.broadcasted_iota(jnp.int32, (rows, held), 1)
        hit = atom.astype(jnp.int32) * num_funcs + row % num_funcs == column
        select = jnp.where(hit, 1.0, 0.0).astype(jnp.bfloat16)
        values = coeff_ref[...].reshape(held, columns)
        step = piece_slots * num_funcs
        for piece, out_ref in enumerate(out_refs):
            result = dot_nn(select[piece * step : (piece + 1) * step], values)
            out_ref[...] = result.astype(jnp.bfloat16).reshape(piece_slots, num_funcs, columns)

    count = num_clusters // 2
    return pl.pallas_call(
        kernel,
        out_shape=[jax.ShapeDtypeStruct((piece_slots, num_funcs, columns), coeff.dtype)] * count,
        in_specs=[SMEM, VMEM, VMEM],
        out_specs=[VMEM] * count,
        compiler_params=PARAMS,
        name="outgoing",
    )(my_cluster.reshape(1), intersection, coeff)


def packed(places, capacity, pieces, direct, relayed, half, carried=None):
    num_funcs, columns = relayed.shape[1:]
    count = len(pieces)
    shape = jax.ShapeDtypeStruct((half, num_funcs, columns), relayed.dtype)

    def kernel(*refs):
        place_ref = refs[0]
        direct_refs = refs[1 : 1 + count]
        relayed_ref = refs[1 + count]
        outs = refs[-1:] if carried is not None else refs[-2:]
        for at, piece in enumerate(pieces):
            for core in range(2):
                for slot in range(capacity):
                    place = place_ref[(2 * piece + core) * capacity + slot]
                    from_ref, index = (direct_refs[at], slot) if core == 0 else (relayed_ref, at * capacity + slot)

                    if carried is None:

                        @pl.when(place < half)
                        def _(place=place, from_ref=from_ref, index=index):
                            outs[0][place] = from_ref[index]

                    @pl.when(jnp.logical_and(place >= half, place < 2 * half))
                    def _(place=place, from_ref=from_ref, index=index):
                        outs[-1][place - half] = from_ref[index]

    operands = [places, *direct, relayed]
    aliases = {}
    if carried is not None:
        operands.append(carried)
        aliases = {len(operands) - 1: 0}
    return pl.pallas_call(
        kernel,
        out_shape=shape if carried is not None else [shape, shape],
        in_specs=[SMEM] + [VMEM] * (len(operands) - 1),
        out_specs=VMEM if carried is not None else [VMEM, VMEM],
        input_output_aliases=aliases,
        compiler_params=PARAMS,
        name="packed",
    )(*operands)


def screened_factors(coulomb, reach, by_step, norm_factor):
    half_stops = (coulomb.shape[1] - 1) // 2
    points = coulomb.shape[0]
    my_reach = reach[0]
    factors = []
    for step in sorted(by_step):
        total = jnp.zeros((points, coulomb.shape[2]), jnp.float32)
        for offset in by_step[step]:
            tile = coulomb[:, offset + half_stops, :].astype(jnp.float32)
            total = total + jnp.where(abs(offset) <= my_reach, tile, jnp.float32(0.0))
        factors.append(total * norm_factor)
    return factors


def two_blocks(coeff, intersection, basis_vals, factors, capacity):
    num_clusters, list_len = intersection.shape
    atom_count, num_funcs, columns = coeff.shape
    my_cluster = lax.axis_index("cluster")
    my_block = lax.axis_index("blk")
    half = list_len // 2
    pieces = outgoing_pieces(coeff, intersection, my_cluster, capacity)
    count = len(pieces)
    first = list(range(3 * count // 4))
    last = list(range(3 * count // 4, count))
    arrived = [pieces[0]] + [swapped(pieces[m], "cluster", 2 * m) for m in range(1, count)]

    my_row = lax.dynamic_index_in_dim(intersection, my_cluster, 0, keepdims=False)
    turn = jnp.bitwise_xor(my_row // atom_count, my_cluster)
    key = turn * list_len + jnp.arange(list_len)
    place = jnp.sum((key[None, :] < key[:, None]).astype(jnp.int32), axis=1)
    turns = jnp.arange(num_clusters)
    begin = jnp.sum((turn[None, :] < turns[:, None]).astype(jnp.int32), axis=1)
    end = jnp.sum((turn[None, :] <= turns[:, None]).astype(jnp.int32), axis=1)
    places = begin[:, None] + jnp.arange(capacity)[None, :]
    places = jnp.where(places < end[:, None], places, list_len).reshape(-1)

    def relay(group):
        return swapped(jnp.concatenate([arrived[m][capacity:] for m in group], axis=0), "cluster", 1)

    relayed = relay(first)
    low, high = packed(places, capacity, first, [arrived[m] for m in first], relayed, half)
    low_other = swapped(low, "blk", 1)
    relayed = relay(last)
    high = packed(places, capacity, last, [arrived[m] for m in last], relayed, half, high)
    high_other = swapped(high, "blk", 1)

    func = jnp.arange(list_len * num_funcs) % num_funcs
    target = jnp.repeat(place, num_funcs) * num_funcs + func
    order = (target[:, None] == jnp.arange(list_len * num_funcs)[None, :]).astype(jnp.bfloat16)
    mine = dot_nn(basis_vals, order).astype(jnp.bfloat16)
    sources = [mine, swapped(mine, "blk", 1)]
    gram = own_gram([low, high])
    offsets = jnp.stack([my_block, 1 - my_block])
    return exchange(offsets, sources, factors, gram, [[low, high], [low_other, high_other]], 2 * columns)


def many_blocks(coeff, intersection, basis_vals, factors, capacity, steps):
    num_clusters, list_len = intersection.shape
    atom_count, num_funcs, columns = coeff.shape
    my_cluster = lax.axis_index("cluster")
    num_blocks = lax.axis_size("blk")
    local_atom = intersection - my_cluster * atom_count
    mine = jnp.logical_and(local_atom >= 0, local_atom < atom_count)
    earlier = jnp.arange(list_len)[:, None] < jnp.arange(list_len)[None, :]
    rank = dot_nn(mine.astype(jnp.bfloat16), earlier.astype(jnp.bfloat16)).astype(jnp.int32)
    matches = jnp.logical_and(mine[:, None, :], rank[:, None, :] == jnp.arange(capacity)[None, :, None])
    source_rows = jnp.sum(jnp.where(matches, local_atom[:, None, :], 0), axis=2)
    outgoing = coeff.at[source_rows.reshape(-1)].get(mode="promise_in_bounds")
    outgoing = outgoing.reshape(num_clusters, capacity, num_funcs, columns)
    incoming = lax.all_to_all(outgoing, "cluster", split_axis=0, concat_axis=0, tiled=True)
    my_row = lax.dynamic_index_in_dim(intersection, my_cluster, 0, keepdims=False)
    my_owners = my_row // atom_count
    same = jnp.logical_and(my_owners[:, None] == my_owners[None, :], earlier.T)
    positions = my_owners * capacity + jnp.sum(same.astype(jnp.int32), axis=1)
    needed = incoming.reshape(num_clusters * capacity, num_funcs, columns)
    needed = needed.at[positions].get(mode="promise_in_bounds")
    needed = needed.reshape(list_len * num_funcs, columns)
    all_columns = lax.all_gather(needed, "blk", axis=1, tiled=True)
    sources = [basis_vals if step == 0 else passed_along(basis_vals, "blk", -step) for step in steps]
    offsets = jnp.zeros((1,), jnp.int32)
    return exchange(offsets, sources, factors, None, [[all_columns]], num_blocks * columns)


def on_device(coeff, intersection, basis_vals, coulomb, reach):
    num_clusters = lax.axis_size("cluster")
    num_blocks = lax.axis_size("blk")
    list_len = intersection.shape[1]
    capacity = 2 * list_len // num_clusters
    half_stops = (coulomb.shape[1] - 1) // 2
    by_step = {}
    for offset in range(-half_stops, half_stops + 1):
        by_step.setdefault(offset % num_blocks, []).append(offset)
    factors = screened_factors(coulomb, reach, by_step, (coeff.shape[2] * num_blocks) ** (-0.5))
    if num_blocks == 2 and num_clusters >= 8 and num_clusters & (num_clusters - 1) == 0:
        return two_blocks(coeff, intersection, basis_vals, factors, capacity)
    return many_blocks(coeff, intersection, basis_vals, factors, capacity, sorted(by_step))


def solution(mesh):
    return jax.shard_map(
        on_device,
        mesh=mesh,
        in_specs=(
            P("cluster", None, "blk"),
            P(),
            P(("cluster", "blk"), None),
            P(("cluster", "blk"), None, None),
            P(("cluster", "blk")),
        ),
        out_specs=P(("cluster", "blk"), None),
        check_vma=False,
    )
```

```python
import jax
import jax.numpy as jnp
from jax import lax
from jax.experimental import pallas as pl
from jax.experimental.pallas import tpu as pltpu
from jax.sharding import PartitionSpec as P


VMEM = pl.BlockSpec(memory_space=pltpu.VMEM)
SMEM = pl.BlockSpec(memory_space=pltpu.SMEM)
PARAMS = pltpu.CompilerParams(vmem_limit_bytes=16 * 2**20)


def passed_along(value, axis, steps):
    count = lax.axis_size(axis)
    pairs = [(source, (source + steps) % count) for source in range(count)]
    return lax.ppermute(value, axis, pairs)


def swapped(value, axis, bits):
    count = lax.axis_size(axis)
    return lax.ppermute(value, axis, [(source, source ^ bits) for source in range(count)])


def split_high_low(value):
    high = value.astype(jnp.bfloat16)
    low = (value - high.astype(jnp.float32)).astype(jnp.bfloat16)
    return high, low


def dot_nn(a, b):
    return lax.dot_general(a, b, (((1,), (0,)), ((), ())), preferred_element_type=jnp.float32)


def dot_nt(a, b):
    return lax.dot_general(a, b, (((1,), (1,)), ((), ())), preferred_element_type=jnp.float32)


def stacked(refs):
    values = [ref[...].reshape(-1, ref.shape[-1]) for ref in refs]
    return values[0] if len(values) == 1 else jnp.concatenate(values, axis=0)


def exchange(offsets, sources, factors, gram, parts, width):
    num_sources = len(sources)
    counts = [len(blocks) for blocks in parts]
    points = sources[0].shape[0]

    def kernel(*refs):
        offset_ref = refs[0]
        basis_refs = refs[1 : 1 + num_sources]
        factor_refs = refs[1 + num_sources : 1 + 2 * num_sources]
        rest = list(refs[1 + 2 * num_sources :])
        total = rest.pop(0)[...] if gram is not None else None
        part_values = []
        for count in counts:
            part_values.append(stacked(rest[:count]))
            rest = rest[count:]
        out_ref = rest[0]
        for values in part_values[0 if gram is None else 1 :]:
            term = dot_nt(values, values)
            total = term if total is None else total + term
        gram_high, gram_low = split_high_low(total)
        own = basis_refs[0][...]
        projected = dot_nn(own, gram_high) + dot_nn(own, gram_low)
        proj_high, proj_low = split_high_low(projected)
        mixed = None
        for source in range(num_sources):
            basis = basis_refs[source][...]
            density = dot_nt(proj_high, basis) + dot_nt(proj_low, basis)
            tile = (density * factor_refs[source][...]).astype(jnp.bfloat16)
            term = dot_nn(tile, basis)
            mixed = term if mixed is None else mixed + term
        mixed_high, mixed_low = split_high_low(mixed)
        for part, values in enumerate(part_values):
            columns = values.shape[1]
            result = dot_nn(mixed_high, values) + dot_nn(mixed_low, values)
            start = pl.multiple_of(offset_ref[part] * columns, columns)
            out_ref[:, pl.ds(start, columns)] = result.astype(out_ref.dtype)

    operands = [offsets, *sources, *factors]
    if gram is not None:
        operands.append(gram)
    for blocks in parts:
        operands.extend(blocks)
    return pl.pallas_call(
        kernel,
        out_shape=jax.ShapeDtypeStruct((points, width), jnp.bfloat16),
        in_specs=[SMEM] + [VMEM] * (len(operands) - 1),
        out_specs=VMEM,
        compiler_params=PARAMS,
        name="exchange",
    )(*operands)


def own_gram(blocks):
    rows = sum(block.shape[0] * block.shape[1] for block in blocks)

    def kernel(*refs):
        values = stacked(refs[:-1])
        refs[-1][...] = dot_nt(values, values)

    return pl.pallas_call(
        kernel,
        out_shape=jax.ShapeDtypeStruct((rows, rows), jnp.float32),
        in_specs=[VMEM] * len(blocks),
        out_specs=VMEM,
        compiler_params=PARAMS,
        name="own_gram",
    )(*blocks)


def outgoing_pieces(coeff, intersection, my_cluster, capacity):
    num_clusters, list_len = intersection.shape
    atom_count, num_funcs, columns = coeff.shape
    slots = num_clusters * capacity
    piece_slots = 2 * capacity
    lanes = 128

    def kernel(me_ref, list_ref, coeff_ref, *out_refs):
        me = me_ref[0]
        local = list_ref[...] - me * atom_count
        mine = jnp.logical_and(local >= 0, local < atom_count)
        ks = lax.broadcasted_iota(jnp.int32, (list_len, list_len), 0)
        ls = lax.broadcasted_iota(jnp.int32, (list_len, list_len), 1)
        earlier = jnp.where(ks < ls, 1.0, 0.0).astype(jnp.bfloat16)
        mine_f = jnp.where(mine, 1.0, 0.0)
        rank = dot_nn(mine_f.astype(jnp.bfloat16), earlier)
        local_f = local.astype(jnp.float32)
        lane = lax.broadcasted_iota(jnp.int32, (num_clusters, lanes), 1)
        source = jnp.zeros((num_clusters, lanes), jnp.float32)
        for slot in range(capacity):
            chosen = jnp.where(jnp.logical_and(mine, rank == slot), local_f, 0.0)
            source = jnp.where(lane == slot, jnp.sum(chosen, axis=1, keepdims=True), source)
        rows = slots * num_funcs
        row = lax.broadcasted_iota(jnp.int32, (rows, num_clusters), 0)
        cluster = lax.broadcasted_iota(jnp.int32, (rows, num_clusters), 1)
        pick = jnp.where(cluster == jnp.bitwise_xor(row // (capacity * num_funcs), me), 1.0, 0.0)
        spread = dot_nn(pick.astype(jnp.bfloat16), source.astype(jnp.bfloat16))
        row = lax.broadcasted_iota(jnp.int32, (rows, lanes), 0)
        lane = lax.broadcasted_iota(jnp.int32, (rows, lanes), 1)
        spread = jnp.where(lane == (row // num_funcs) % capacity, spread, 0.0)
        held = atom_count * num_funcs
        atom = dot_nn(spread.astype(jnp.bfloat16), jnp.ones((lanes, held), jnp.bfloat16))
        row = lax.broadcasted_iota(jnp.int32, (rows, held), 0)
        column = lax.broadcasted_iota(jnp.int32, (rows, held), 1)
        hit = atom.astype(jnp.int32) * num_funcs + row % num_funcs == column
        select = jnp.where(hit, 1.0, 0.0).astype(jnp.bfloat16)
        values = coeff_ref[...].reshape(held, columns)
        step = piece_slots * num_funcs
        for piece, out_ref in enumerate(out_refs):
            result = dot_nn(select[piece * step : (piece + 1) * step], values)
            out_ref[...] = result.astype(jnp.bfloat16).reshape(piece_slots, num_funcs, columns)

    count = num_clusters // 2
    return pl.pallas_call(
        kernel,
        out_shape=[jax.ShapeDtypeStruct((piece_slots, num_funcs, columns), coeff.dtype)] * count,
        in_specs=[SMEM, VMEM, VMEM],
        out_specs=[VMEM] * count,
        compiler_params=PARAMS,
        name="outgoing",
    )(my_cluster.reshape(1), intersection, coeff)


def packed(places, capacity, pieces, direct, relayed, half, carried=None):
    num_funcs, columns = relayed[0].shape[1:]
    count = len(pieces)
    shape = jax.ShapeDtypeStruct((half, num_funcs, columns), relayed[0].dtype)

    def kernel(*refs):
        place_ref = refs[0]
        direct_refs = refs[1 : 1 + count]
        relayed_refs = refs[1 + count : 1 + 2 * count]
        outs = refs[-1:] if carried is not None else refs[-2:]
        for at, piece in enumerate(pieces):
            for core in range(2):
                for slot in range(capacity):
                    place = place_ref[(2 * piece + core) * capacity + slot]
                    from_ref = direct_refs[at] if core == 0 else relayed_refs[at]

                    if carried is None:

                        @pl.when(place < half)
                        def _(place=place, from_ref=from_ref, slot=slot):
                            outs[0][place] = from_ref[slot]

                    @pl.when(jnp.logical_and(place >= half, place < 2 * half))
                    def _(place=place, from_ref=from_ref, slot=slot):
                        outs[-1][place - half] = from_ref[slot]

    operands = [places, *direct, *relayed]
    aliases = {}
    if carried is not None:
        operands.append(carried)
        aliases = {len(operands) - 1: 0}
    return pl.pallas_call(
        kernel,
        out_shape=shape if carried is not None else [shape, shape],
        in_specs=[SMEM] + [VMEM] * (len(operands) - 1),
        out_specs=VMEM if carried is not None else [VMEM, VMEM],
        input_output_aliases=aliases,
        compiler_params=PARAMS,
        name="packed",
    )(*operands)


def screened_factors(coulomb, reach, by_step, norm_factor):
    half_stops = (coulomb.shape[1] - 1) // 2
    points = coulomb.shape[0]
    my_reach = reach[0]
    factors = []
    for step in sorted(by_step):
        total = jnp.zeros((points, coulomb.shape[2]), jnp.float32)
        for offset in by_step[step]:
            tile = coulomb[:, offset + half_stops, :].astype(jnp.float32)
            total = total + jnp.where(abs(offset) <= my_reach, tile, jnp.float32(0.0))
        factors.append(total * norm_factor)
    return factors


def two_blocks(coeff, intersection, basis_vals, factors, capacity):
    num_clusters, list_len = intersection.shape
    atom_count, num_funcs, columns = coeff.shape
    my_cluster = lax.axis_index("cluster")
    my_block = lax.axis_index("blk")
    half = list_len // 2
    pieces = outgoing_pieces(coeff, intersection, my_cluster, capacity)
    count = len(pieces)
    first = list(range(3 * count // 4))
    last = list(range(3 * count // 4, count))
    arrived = [pieces[0]]
    for m in range(1, count):
        arrived.append(swapped(pieces[m], "cluster", 2 * m))

    later, _ = lax.optimization_barrier((intersection, pieces[0]))
    my_row = lax.dynamic_index_in_dim(later, my_cluster, 0, keepdims=False)
    turn = jnp.bitwise_xor(my_row // atom_count, my_cluster)
    key = turn * list_len + jnp.arange(list_len)
    place = jnp.sum((key[None, :] < key[:, None]).astype(jnp.int32), axis=1)
    func = jnp.arange(list_len * num_funcs) % num_funcs
    target = jnp.repeat(place, num_funcs) * num_funcs + func
    order = (target[:, None] == jnp.arange(list_len * num_funcs)[None, :]).astype(jnp.bfloat16)
    mine = dot_nn(basis_vals, order).astype(jnp.bfloat16)

    turns = jnp.arange(num_clusters)
    begin = jnp.sum((turn[None, :] < turns[:, None]).astype(jnp.int32), axis=1)
    end = jnp.sum((turn[None, :] <= turns[:, None]).astype(jnp.int32), axis=1)
    places = begin[:, None] + jnp.arange(capacity)[None, :]
    places = jnp.where(places < end[:, None], places, list_len).reshape(-1)

    sources = [mine, swapped(mine, "blk", 1)]

    relayed = []
    for m in range(count):
        relayed.append(swapped(arrived[m][capacity:], "cluster", 1))

    def group(values, at):
        return [values[m] for m in at]

    low, high = packed(places, capacity, first, group(arrived, first), group(relayed, first), half)
    low_other = swapped(low, "blk", 1)
    high = packed(places, capacity, last, group(arrived, last), group(relayed, last), half, high)
    high_other = swapped(high, "blk", 1)
    gram = own_gram([low, high])
    offsets = jnp.stack([my_block, 1 - my_block])
    return exchange(offsets, sources, factors, gram, [[low, high], [low_other, high_other]], 2 * columns)


def many_blocks(coeff, intersection, basis_vals, factors, capacity, steps):
    num_clusters, list_len = intersection.shape
    atom_count, num_funcs, columns = coeff.shape
    my_cluster = lax.axis_index("cluster")
    num_blocks = lax.axis_size("blk")
    local_atom = intersection - my_cluster * atom_count
    mine = jnp.logical_and(local_atom >= 0, local_atom < atom_count)
    earlier = jnp.arange(list_len)[:, None] < jnp.arange(list_len)[None, :]
    rank = dot_nn(mine.astype(jnp.bfloat16), earlier.astype(jnp.bfloat16)).astype(jnp.int32)
    matches = jnp.logical_and(mine[:, None, :], rank[:, None, :] == jnp.arange(capacity)[None, :, None])
    source_rows = jnp.sum(jnp.where(matches, local_atom[:, None, :], 0), axis=2)
    outgoing = coeff.at[source_rows.reshape(-1)].get(mode="promise_in_bounds")
    outgoing = outgoing.reshape(num_clusters, capacity, num_funcs, columns)
    incoming = lax.all_to_all(outgoing, "cluster", split_axis=0, concat_axis=0, tiled=True)
    my_row = lax.dynamic_index_in_dim(intersection, my_cluster, 0, keepdims=False)
    my_owners = my_row // atom_count
    same = jnp.logical_and(my_owners[:, None] == my_owners[None, :], earlier.T)
    positions = my_owners * capacity + jnp.sum(same.astype(jnp.int32), axis=1)
    needed = incoming.reshape(num_clusters * capacity, num_funcs, columns)
    needed = needed.at[positions].get(mode="promise_in_bounds")
    needed = needed.reshape(list_len * num_funcs, columns)
    all_columns = lax.all_gather(needed, "blk", axis=1, tiled=True)
    sources = [basis_vals if step == 0 else passed_along(basis_vals, "blk", -step) for step in steps]
    offsets = jnp.zeros((1,), jnp.int32)
    return exchange(offsets, sources, factors, None, [[all_columns]], num_blocks * columns)


def on_device(coeff, intersection, basis_vals, coulomb, reach):
    num_clusters = lax.axis_size("cluster")
    num_blocks = lax.axis_size("blk")
    list_len = intersection.shape[1]
    capacity = 2 * list_len // num_clusters
    half_stops = (coulomb.shape[1] - 1) // 2
    by_step = {}
    for offset in range(-half_stops, half_stops + 1):
        by_step.setdefault(offset % num_blocks, []).append(offset)
    factors = screened_factors(coulomb, reach, by_step, (coeff.shape[2] * num_blocks) ** (-0.5))
    if takes_two_blocks(num_clusters, num_blocks):
        return two_blocks(coeff, intersection, basis_vals, factors, capacity)
    return many_blocks(coeff, intersection, basis_vals, factors, capacity, sorted(by_step))


def takes_two_blocks(num_clusters, num_blocks):
    return num_blocks == 2 and num_clusters >= 16 and num_clusters & (num_clusters - 1) == 0


def solution(mesh):
    return jax.shard_map(
        on_device,
        mesh=mesh,
        in_specs=(
            P("cluster", None, "blk"),
            P(),
            P(("cluster", "blk"), None),
            P(("cluster", "blk"), None, None),
            P(("cluster", "blk")),
        ),
        out_specs=P(("cluster", "blk"), None),
        check_vma=False,
    )
```

```python
import jax
import jax.numpy as jnp
from jax import lax
from jax.experimental import pallas as pl
from jax.experimental.pallas import tpu as pltpu
from jax.sharding import PartitionSpec as P


EARLY_PARTS = 5

VMEM = pl.BlockSpec(memory_space=pltpu.VMEM)
SMEM = pl.BlockSpec(memory_space=pltpu.SMEM)
ANY = pl.BlockSpec(memory_space=pl.ANY)
PARAMS = pltpu.CompilerParams(vmem_limit_bytes=16 * 2**20)


def passed_along(value, axis, steps):
    count = lax.axis_size(axis)
    pairs = [(source, (source + steps) % count) for source in range(count)]
    return lax.ppermute(value, axis, pairs)


def swapped(value, axis, bits):
    count = lax.axis_size(axis)
    return lax.ppermute(value, axis, [(source, source ^ bits) for source in range(count)])


def split_high_low(value):
    high = value.astype(jnp.bfloat16)
    low = (value - high.astype(jnp.float32)).astype(jnp.bfloat16)
    return high, low


def dot_nn(a, b):
    return lax.dot_general(a, b, (((1,), (0,)), ((), ())), preferred_element_type=jnp.float32)


def dot_nt(a, b):
    return lax.dot_general(a, b, (((1,), (1,)), ((), ())), preferred_element_type=jnp.float32)


def exchange(starts, sources, factors, gram, known, parts, width):
    num_sources = len(sources)
    num_parts = len(parts)
    points = sources[0].shape[0]
    widths = [part.shape[1] for part in parts]

    def kernel(*refs):
        start_ref = refs[0]
        basis_refs = refs[1 : 1 + num_sources]
        factor_refs = refs[1 + num_sources : 1 + 2 * num_sources]
        rest = list(refs[1 + 2 * num_sources :])
        total = rest.pop(0)[...] if gram is not None else None
        part_refs = rest[:num_parts]
        out_ref = rest[num_parts]
        held_refs = rest[num_parts + 1 : 2 * num_parts + 1]
        sems = rest[-1]
        for part in range(known, num_parts):
            values = part_refs[part][...]
            term = dot_nt(values, values)
            total = term if total is None else total + term
        gram_high, gram_low = split_high_low(total)
        own = basis_refs[0][...]
        projected = dot_nn(own, gram_high) + dot_nn(own, gram_low)
        proj_high, proj_low = split_high_low(projected)
        mixed = None
        for source in range(num_sources):
            basis = basis_refs[source][...]
            density = dot_nt(proj_high, basis) + dot_nt(proj_low, basis)
            tile = (density * factor_refs[source][...]).astype(jnp.bfloat16)
            term = dot_nn(tile, basis)
            mixed = term if mixed is None else mixed + term
        mixed_high, mixed_low = split_high_low(mixed)
        copies = []
        for part in range(num_parts):
            values = part_refs[part][...]
            result = dot_nn(mixed_high, values) + dot_nn(mixed_low, values)
            held_refs[part][...] = result.astype(out_ref.dtype)
            start = pl.multiple_of(start_ref[part] * 128, 128)
            copy = pltpu.make_async_copy(held_refs[part], out_ref.at[:, pl.ds(start, widths[part])], sems.at[part])
            copy.start()
            copies.append(copy)
        for copy in copies:
            copy.wait()

    operands = [starts, *sources, *factors]
    if gram is not None:
        operands.append(gram)
    operands.extend(parts)
    return pl.pallas_call(
        kernel,
        out_shape=jax.ShapeDtypeStruct((points, width), jnp.bfloat16),
        in_specs=[SMEM] + [VMEM] * (len(operands) - 1),
        out_specs=ANY,
        scratch_shapes=[pltpu.VMEM((points, columns), jnp.bfloat16) for columns in widths]
        + [pltpu.SemaphoreType.DMA((num_parts,))],
        compiler_params=PARAMS,
        name="exchange",
    )(*operands)


def gram_of(values, carried=None):
    rows = values.shape[0]

    def kernel(*refs):
        block = refs[0][...]
        total = dot_nt(block, block)
        refs[-1][...] = total if carried is None else total + refs[1][...]

    operands = [values] if carried is None else [values, carried]
    return pl.pallas_call(
        kernel,
        out_shape=jax.ShapeDtypeStruct((rows, rows), jnp.float32),
        in_specs=[VMEM] * len(operands),
        out_specs=VMEM,
        compiler_params=PARAMS,
        name="gram_of",
    )(*operands)


def outgoing(coeff, intersection, my_cluster, capacity, split):
    num_clusters, list_len = intersection.shape
    atom_count, num_funcs, columns = coeff.shape
    slots = num_clusters * capacity
    held = atom_count * num_funcs
    lanes = 128

    def kernel(me_ref, list_ref, coeff_ref, early_ref, *rest):
        late_refs = rest[: num_clusters // 2]
        list_held, coeff_held, late_held, sems = rest[num_clusters // 2 :]
        coeff_copy = pltpu.make_async_copy(coeff_ref, coeff_held, sems.at[0])
        list_copy = pltpu.make_async_copy(list_ref, list_held, sems.at[1])
        list_copy.start()
        coeff_copy.start()
        me = me_ref[0]
        list_copy.wait()
        local = list_held[...] - me * atom_count
        mine = jnp.logical_and(local >= 0, local < atom_count)
        ks = lax.broadcasted_iota(jnp.int32, (list_len, list_len), 0)
        ls = lax.broadcasted_iota(jnp.int32, (list_len, list_len), 1)
        earlier = jnp.where(ks < ls, 1.0, 0.0).astype(jnp.bfloat16)
        mine_f = jnp.where(mine, 1.0, 0.0)
        rank = dot_nn(mine_f.astype(jnp.bfloat16), earlier)
        local_f = local.astype(jnp.float32)
        lane = lax.broadcasted_iota(jnp.int32, (num_clusters, lanes), 1)
        source = jnp.zeros((num_clusters, lanes), jnp.float32)
        for slot in range(capacity):
            chosen = jnp.where(jnp.logical_and(mine, rank == slot), local_f, 0.0)
            source = jnp.where(lane == slot, jnp.sum(chosen, axis=1, keepdims=True), source)
        rows = slots * num_funcs
        row = lax.broadcasted_iota(jnp.int32, (rows, num_clusters), 0)
        cluster = lax.broadcasted_iota(jnp.int32, (rows, num_clusters), 1)
        pick = jnp.where(cluster == row // (capacity * num_funcs), 1.0, 0.0)
        spread = dot_nn(pick.astype(jnp.bfloat16), source.astype(jnp.bfloat16))
        row = lax.broadcasted_iota(jnp.int32, (rows, lanes), 0)
        lane = lax.broadcasted_iota(jnp.int32, (rows, lanes), 1)
        spread = jnp.where(lane == (row // num_funcs) % capacity, spread, 0.0)
        atom = dot_nn(spread.astype(jnp.bfloat16), jnp.ones((lanes, held), jnp.bfloat16))
        row = lax.broadcasted_iota(jnp.int32, (rows, held), 0)
        column = lax.broadcasted_iota(jnp.int32, (rows, held), 1)
        hit = atom.astype(jnp.int32) * num_funcs + row % num_funcs == column
        select = jnp.where(hit, 1.0, 0.0).astype(jnp.bfloat16)
        coeff_copy.wait()
        values = coeff_held[...].reshape(held, columns)
        result = dot_nn(select, values[:, :split]).astype(jnp.bfloat16)
        early_ref[...] = result.reshape(slots, num_funcs, split)
        result = dot_nn(select, values[:, split:]).astype(jnp.bfloat16)
        late_held[...] = result.reshape(slots, num_funcs, columns - split)
        for turn in range(num_clusters):
            target = jnp.bitwise_xor(me, turn) * capacity
            side = turn % 2 * capacity
            late_refs[turn // 2][side : side + capacity] = late_held[pl.ds(target, capacity)]

    count = num_clusters // 2
    late = jax.ShapeDtypeStruct((2 * capacity, num_funcs, columns - split), coeff.dtype)
    return pl.pallas_call(
        kernel,
        out_shape=[jax.ShapeDtypeStruct((slots, num_funcs, split), coeff.dtype)] + [late] * count,
        in_specs=[SMEM, ANY, ANY],
        out_specs=[VMEM] * (count + 1),
        scratch_shapes=[
            pltpu.VMEM((num_clusters, list_len), jnp.int32),
            pltpu.VMEM(coeff.shape, coeff.dtype),
            pltpu.VMEM((slots, num_funcs, columns - split), coeff.dtype),
            pltpu.SemaphoreType.DMA((2,)),
        ],
        compiler_params=PARAMS,
        name="outgoing",
    )(my_cluster.reshape(1), intersection, coeff)


def packed(positions, blocks):
    list_len = positions.shape[0]
    num_funcs, columns = blocks[0].shape[1:]
    slots = sum(block.shape[0] for block in blocks)

    def kernel(position_ref, *rest):
        block_refs = rest[: len(blocks)]
        out_ref = rest[len(blocks)]
        if len(blocks) > 1:
            held_ref = rest[-1]
            begin = 0
            for ref in block_refs:
                held_ref[begin : begin + ref.shape[0]] = ref[...]
                begin += ref.shape[0]
        else:
            held_ref = block_refs[0]
        for k in range(list_len):
            out_ref[k] = held_ref[position_ref[k]]

    return pl.pallas_call(
        kernel,
        out_shape=jax.ShapeDtypeStruct((list_len, num_funcs, columns), blocks[0].dtype),
        in_specs=[SMEM] + [VMEM] * len(blocks),
        out_specs=VMEM,
        scratch_shapes=[pltpu.VMEM((slots, num_funcs, columns), blocks[0].dtype)] if len(blocks) > 1 else [],
        compiler_params=PARAMS,
        name="packed",
    )(positions, *blocks).reshape(list_len * num_funcs, columns)


def screened_factors(coulomb, reach, by_step, norm_factor):
    half_stops = (coulomb.shape[1] - 1) // 2
    points = coulomb.shape[0]
    my_reach = reach[0]
    factors = []
    for step in sorted(by_step):
        total = jnp.zeros((points, coulomb.shape[2]), jnp.float32)
        for offset in by_step[step]:
            tile = coulomb[:, offset + half_stops, :].astype(jnp.float32)
            total = total + jnp.where(abs(offset) <= my_reach, tile, jnp.float32(0.0))
        factors.append(total * norm_factor)
    return factors


def two_blocks(coeff, intersection, basis_vals, factors, capacity):
    num_clusters, list_len = intersection.shape
    atom_count, num_funcs, columns = coeff.shape
    my_cluster = lax.axis_index("cluster")
    my_block = lax.axis_index("blk")
    split = max(columns * EARLY_PARTS // 8 // 128, 1) * 128
    early, *pieces = outgoing(coeff, intersection, my_cluster, capacity, split)
    early = early.reshape(num_clusters, capacity, num_funcs, split)
    early = lax.all_to_all(early, "cluster", split_axis=0, concat_axis=0, tiled=True)
    early = early.reshape(num_clusters * capacity, num_funcs, split)
    arrived = [pieces[0]]
    for m in range(1, len(pieces)):
        arrived.append(swapped(pieces[m], "cluster", 2 * m))
    relayed = []
    for m in range(len(pieces)):
        relayed.append(swapped(arrived[m][capacity:], "cluster", 1))
    sources = [basis_vals, swapped(basis_vals, "blk", 1)]

    later, _ = lax.optimization_barrier((intersection, pieces[0]))
    my_row = lax.dynamic_index_in_dim(later, my_cluster, 0, keepdims=False)
    owner = my_row // atom_count
    same = jnp.logical_and(owner[:, None] == owner[None, :], jnp.arange(list_len)[:, None] > jnp.arange(list_len)[None, :])
    rank = jnp.sum(same.astype(jnp.int32), axis=1)
    turn = jnp.bitwise_xor(owner, my_cluster)
    early_at = owner * capacity + rank
    late_at = turn // 2 * capacity + rank + jnp.where(turn % 2 == 1, num_clusters // 2 * capacity, 0)

    early = packed(early_at, [early])
    early_other = swapped(early, "blk", 1)
    gram = gram_of(early)
    late = packed(late_at, [piece[:capacity] for piece in arrived] + relayed)
    late_other = swapped(late, "blk", 1)
    gram = gram_of(late, gram)
    gram = gram_of(early_other, gram)
    lanes = columns // 128
    begin = jnp.stack([my_block * lanes, (1 - my_block) * lanes])
    starts = (begin[None, :] + jnp.array([0, split // 128])[:, None]).reshape(-1)
    return exchange(starts, sources, factors, gram, 3, [early, early_other, late, late_other], 2 * columns)


def many_blocks(coeff, intersection, basis_vals, factors, capacity, steps):
    num_clusters, list_len = intersection.shape
    atom_count, num_funcs, columns = coeff.shape
    my_cluster = lax.axis_index("cluster")
    num_blocks = lax.axis_size("blk")
    local_atom = intersection - my_cluster * atom_count
    mine = jnp.logical_and(local_atom >= 0, local_atom < atom_count)
    earlier = jnp.arange(list_len)[:, None] < jnp.arange(list_len)[None, :]
    rank = dot_nn(mine.astype(jnp.bfloat16), earlier.astype(jnp.bfloat16)).astype(jnp.int32)
    matches = jnp.logical_and(mine[:, None, :], rank[:, None, :] == jnp.arange(capacity)[None, :, None])
    source_rows = jnp.sum(jnp.where(matches, local_atom[:, None, :], 0), axis=2)
    outgoing = coeff.at[source_rows.reshape(-1)].get(mode="promise_in_bounds")
    outgoing = outgoing.reshape(num_clusters, capacity, num_funcs, columns)
    incoming = lax.all_to_all(outgoing, "cluster", split_axis=0, concat_axis=0, tiled=True)
    my_row = lax.dynamic_index_in_dim(intersection, my_cluster, 0, keepdims=False)
    my_owners = my_row // atom_count
    same = jnp.logical_and(my_owners[:, None] == my_owners[None, :], earlier.T)
    positions = my_owners * capacity + jnp.sum(same.astype(jnp.int32), axis=1)
    needed = incoming.reshape(num_clusters * capacity, num_funcs, columns)
    needed = needed.at[positions].get(mode="promise_in_bounds")
    needed = needed.reshape(list_len * num_funcs, columns)
    all_columns = lax.all_gather(needed, "blk", axis=1, tiled=True)
    sources = [basis_vals if step == 0 else passed_along(basis_vals, "blk", -step) for step in steps]
    starts = jnp.zeros((1,), jnp.int32)
    return exchange(starts, sources, factors, None, 0, [all_columns], num_blocks * columns)


def on_device(coeff, intersection, basis_vals, coulomb, reach):
    num_clusters = lax.axis_size("cluster")
    num_blocks = lax.axis_size("blk")
    list_len = intersection.shape[1]
    capacity = 2 * list_len // num_clusters
    half_stops = (coulomb.shape[1] - 1) // 2
    by_step = {}
    for offset in range(-half_stops, half_stops + 1):
        by_step.setdefault(offset % num_blocks, []).append(offset)
    factors = screened_factors(coulomb, reach, by_step, (coeff.shape[2] * num_blocks) ** (-0.5))
    if takes_two_blocks(num_clusters, num_blocks):
        return two_blocks(coeff, intersection, basis_vals, factors, capacity)
    return many_blocks(coeff, intersection, basis_vals, factors, capacity, sorted(by_step))


def takes_two_blocks(num_clusters, num_blocks):
    return num_blocks == 2 and num_clusters >= 16 and num_clusters & (num_clusters - 1) == 0


def solution(mesh):
    return jax.shard_map(
        on_device,
        mesh=mesh,
        in_specs=(
            P("cluster", None, "blk"),
            P(),
            P(("cluster", "blk"), None),
            P(("cluster", "blk"), None, None),
            P(("cluster", "blk")),
        ),
        out_specs=P(("cluster", "blk"), None),
        check_vma=False,
    )
```

```python
import jax
import jax.numpy as jnp
from jax import lax
from jax.experimental import pallas as pl
from jax.experimental.pallas import tpu as pltpu
from jax.sharding import PartitionSpec as P


EARLY_PARTS = 5

VMEM = pl.BlockSpec(memory_space=pltpu.VMEM)
SMEM = pl.BlockSpec(memory_space=pltpu.SMEM)
HBM = pl.BlockSpec(memory_space=pltpu.HBM)
PARAMS = pltpu.CompilerParams(vmem_limit_bytes=12 * 2**20)


def passed_along(value, axis, steps):
    count = lax.axis_size(axis)
    pairs = [(source, (source + steps) % count) for source in range(count)]
    return lax.ppermute(value, axis, pairs)


def swapped(value, axis, bits):
    count = lax.axis_size(axis)
    return lax.ppermute(value, axis, [(source, source ^ bits) for source in range(count)])


def split_high_low(value):
    high = value.astype(jnp.bfloat16)
    low = (value - high.astype(jnp.float32)).astype(jnp.bfloat16)
    return high, low


def dot_nn(a, b):
    return lax.dot_general(a, b, (((1,), (0,)), ((), ())), preferred_element_type=jnp.float32)


def dot_nt(a, b):
    return lax.dot_general(a, b, (((1,), (1,)), ((), ())), preferred_element_type=jnp.float32)


def exchange(starts, sources, factors, gram, known, parts, width):
    num_sources = len(sources)
    num_parts = len(parts)
    points = sources[0].shape[0]
    widths = [part.shape[1] for part in parts]

    def kernel(*refs):
        start_ref = refs[0]
        basis_refs = refs[1 : 1 + num_sources]
        factor_refs = refs[1 + num_sources : 1 + 2 * num_sources]
        rest = list(refs[1 + 2 * num_sources :])
        total = rest.pop(0)[...] if gram is not None else None
        part_refs = rest[:num_parts]
        out_ref = rest[num_parts]
        held_refs = rest[num_parts + 1 : 2 * num_parts + 1]
        sems = rest[-1]
        for part in range(known, num_parts):
            values = part_refs[part][...]
            term = dot_nt(values, values)
            total = term if total is None else total + term
        gram_high, gram_low = split_high_low(total)
        own = basis_refs[0][...]
        projected = dot_nn(own, gram_high) + dot_nn(own, gram_low)
        proj_high, proj_low = split_high_low(projected)
        mixed = None
        for source in range(num_sources):
            basis = basis_refs[source][...]
            density = dot_nt(proj_high, basis) + dot_nt(proj_low, basis)
            tile = (density * factor_refs[source][...]).astype(jnp.bfloat16)
            term = dot_nn(tile, basis)
            mixed = term if mixed is None else mixed + term
        mixed_high, mixed_low = split_high_low(mixed)
        copies = []
        for part in range(num_parts):
            values = part_refs[part][...]
            result = dot_nn(mixed_high, values) + dot_nn(mixed_low, values)
            held_refs[part][...] = result.astype(out_ref.dtype)
            start = pl.multiple_of(start_ref[part] * 128, 128)
            copy = pltpu.make_async_copy(held_refs[part], out_ref.at[:, pl.ds(start, widths[part])], sems.at[part])
            copy.start()
            copies.append(copy)
        for copy in copies:
            copy.wait()

    operands = [starts, *sources, *factors]
    if gram is not None:
        operands.append(gram)
    operands.extend(parts)
    return pl.pallas_call(
        kernel,
        out_shape=jax.ShapeDtypeStruct((points, width), jnp.bfloat16),
        in_specs=[SMEM] + [VMEM] * (len(operands) - 1),
        out_specs=HBM,
        scratch_shapes=[pltpu.VMEM((points, columns), jnp.bfloat16) for columns in widths]
        + [pltpu.SemaphoreType.DMA((num_parts,))],
        compiler_params=PARAMS,
        name="exchange",
    )(*operands)


def gram_of(values, carried=None):
    rows = values.shape[0]

    def kernel(*refs):
        block = refs[0][...]
        total = dot_nt(block, block)
        refs[-1][...] = total if carried is None else total + refs[1][...]

    operands = [values] if carried is None else [values, carried]
    return pl.pallas_call(
        kernel,
        out_shape=jax.ShapeDtypeStruct((rows, rows), jnp.float32),
        in_specs=[VMEM] * len(operands),
        out_specs=VMEM,
        compiler_params=PARAMS,
        name="gram_of",
    )(*operands)


def outgoing(coeff, intersection, my_cluster, capacity, split):
    num_clusters, list_len = intersection.shape
    atom_count, num_funcs, columns = coeff.shape
    slots = num_clusters * capacity
    held = atom_count * num_funcs
    lanes = 128

    def kernel(me_ref, list_ref, coeff_ref, list_held, late_ref, *rest):
        early_refs = rest[: num_clusters // 2]
        coeff_held, early_held, sems = rest[num_clusters // 2 :]
        coeff_copy = pltpu.make_async_copy(coeff_ref, coeff_held, sems.at[0])
        list_copy = pltpu.make_async_copy(list_ref, list_held, sems.at[1])
        list_copy.start()
        coeff_copy.start()
        me = me_ref[0]
        list_copy.wait()
        local = list_held[...] - me * atom_count
        mine = jnp.logical_and(local >= 0, local < atom_count)
        ks = lax.broadcasted_iota(jnp.int32, (list_len, list_len), 0)
        ls = lax.broadcasted_iota(jnp.int32, (list_len, list_len), 1)
        earlier = jnp.where(ks < ls, 1.0, 0.0).astype(jnp.bfloat16)
        mine_f = jnp.where(mine, 1.0, 0.0)
        rank = dot_nn(mine_f.astype(jnp.bfloat16), earlier)
        local_f = local.astype(jnp.float32)
        lane = lax.broadcasted_iota(jnp.int32, (num_clusters, lanes), 1)
        source = jnp.zeros((num_clusters, lanes), jnp.float32)
        for slot in range(capacity):
            chosen = jnp.where(jnp.logical_and(mine, rank == slot), local_f, 0.0)
            source = jnp.where(lane == slot, jnp.sum(chosen, axis=1, keepdims=True), source)
        rows = slots * num_funcs
        row = lax.broadcasted_iota(jnp.int32, (rows, num_clusters), 0)
        cluster = lax.broadcasted_iota(jnp.int32, (rows, num_clusters), 1)
        pick = jnp.where(cluster == row // (capacity * num_funcs), 1.0, 0.0)
        spread = dot_nn(pick.astype(jnp.bfloat16), source.astype(jnp.bfloat16))
        row = lax.broadcasted_iota(jnp.int32, (rows, lanes), 0)
        lane = lax.broadcasted_iota(jnp.int32, (rows, lanes), 1)
        spread = jnp.where(lane == (row // num_funcs) % capacity, spread, 0.0)
        atom = dot_nn(spread.astype(jnp.bfloat16), jnp.ones((lanes, held), jnp.bfloat16))
        row = lax.broadcasted_iota(jnp.int32, (rows, held), 0)
        column = lax.broadcasted_iota(jnp.int32, (rows, held), 1)
        hit = atom.astype(jnp.int32) * num_funcs + row % num_funcs == column
        select = jnp.where(hit, 1.0, 0.0).astype(jnp.bfloat16)
        coeff_copy.wait()
        values = coeff_held[...].reshape(held, columns)
        result = dot_nn(select, values[:, :split]).astype(jnp.bfloat16)
        early_held[...] = result.reshape(slots, num_funcs, split)
        for turn in range(num_clusters):
            target = jnp.bitwise_xor(me, turn) * capacity
            side = turn % 2 * capacity
            early_refs[turn // 2][side : side + capacity] = early_held[pl.ds(target, capacity)]
        result = dot_nn(select, values[:, split:]).astype(jnp.bfloat16)
        late_ref[...] = result.reshape(slots, num_funcs, columns - split)

    count = num_clusters // 2
    late = jax.ShapeDtypeStruct((slots, num_funcs, columns - split), coeff.dtype)
    early = jax.ShapeDtypeStruct((2 * capacity, num_funcs, split), coeff.dtype)
    return pl.pallas_call(
        kernel,
        out_shape=[jax.ShapeDtypeStruct(intersection.shape, jnp.int32), late] + [early] * count,
        in_specs=[SMEM, HBM, HBM],
        out_specs=[VMEM] * (count + 2),
        scratch_shapes=[
            pltpu.VMEM(coeff.shape, coeff.dtype),
            pltpu.VMEM((slots, num_funcs, split), coeff.dtype),
            pltpu.SemaphoreType.DMA((2,)),
        ],
        compiler_params=PARAMS,
        name="outgoing",
    )(
        my_cluster.reshape(1),
        pltpu.with_memory_space_constraint(intersection, pltpu.HBM),
        pltpu.with_memory_space_constraint(coeff, pltpu.HBM),
    )


def packed(positions, blocks, taken, last):
    list_len = positions.shape[0]
    num_funcs, columns = last.shape[1:]
    slots = len(blocks) * taken + last.shape[0]

    def kernel(position_ref, *rest):
        last_ref, out_ref = rest[len(blocks) : len(blocks) + 2]
        held_ref = rest[-1] if blocks else last_ref
        if blocks:
            for at, ref in enumerate(rest[: len(blocks)]):
                held_ref[at * taken : (at + 1) * taken] = ref[:taken]
            held_ref[len(blocks) * taken :] = last_ref[...]
        for k in range(list_len):
            out_ref[k] = held_ref[position_ref[k]]

    return pl.pallas_call(
        kernel,
        out_shape=jax.ShapeDtypeStruct((list_len, num_funcs, columns), last.dtype),
        in_specs=[SMEM] + [VMEM] * (len(blocks) + 1),
        out_specs=VMEM,
        scratch_shapes=[pltpu.VMEM((slots, num_funcs, columns), last.dtype)] if blocks else [],
        compiler_params=PARAMS,
        name="packed",
    )(positions, *blocks, last).reshape(list_len * num_funcs, columns)


def screened_factors(coulomb, reach, by_step, norm_factor):
    half_stops = (coulomb.shape[1] - 1) // 2
    points = coulomb.shape[0]
    my_reach = reach[0]
    factors = []
    for step in sorted(by_step):
        total = jnp.zeros((points, coulomb.shape[2]), jnp.float32)
        for offset in by_step[step]:
            tile = coulomb[:, offset + half_stops, :].astype(jnp.float32)
            total = total + jnp.where(abs(offset) <= my_reach, tile, jnp.float32(0.0))
        factors.append(total * norm_factor)
    return factors


def two_blocks(coeff, intersection, basis_vals, factors, capacity):
    num_clusters, list_len = intersection.shape
    atom_count, num_funcs, columns = coeff.shape
    my_cluster = lax.axis_index("cluster")
    my_block = lax.axis_index("blk")
    split = max(columns * EARLY_PARTS // 8 // 128, 1) * 128
    listed, late, *pieces = outgoing(coeff, intersection, my_cluster, capacity, split)
    arrived = [pieces[0]]
    for m in range(1, len(pieces)):
        arrived.append(swapped(pieces[m], "cluster", 2 * m))
    late = late.reshape(num_clusters, capacity, num_funcs, columns - split)
    late = lax.all_to_all(late, "cluster", split_axis=0, concat_axis=0, tiled=True)
    late = late.reshape(num_clusters * capacity, num_funcs, columns - split)
    relayed = swapped(jnp.concatenate([piece[capacity:] for piece in arrived], axis=0), "cluster", 1)
    sources = [basis_vals, swapped(basis_vals, "blk", 1)]

    my_row = lax.dynamic_index_in_dim(listed, my_cluster, 0, keepdims=False)
    owner = my_row // atom_count
    same = jnp.logical_and(owner[:, None] == owner[None, :], jnp.arange(list_len)[:, None] > jnp.arange(list_len)[None, :])
    rank = jnp.sum(same.astype(jnp.int32), axis=1)
    turn = jnp.bitwise_xor(owner, my_cluster)
    early_at = turn // 2 * capacity + rank + jnp.where(turn % 2 == 1, num_clusters // 2 * capacity, 0)
    late_at = owner * capacity + rank

    early = packed(early_at, arrived, capacity, relayed)
    early_other = swapped(early, "blk", 1)
    gram = gram_of(early)
    late = packed(late_at, [], 0, late)
    late_other = swapped(late, "blk", 1)
    gram = gram_of(late, gram)
    gram = gram_of(early_other, gram)
    lanes = columns // 128
    begin = jnp.stack([my_block * lanes, (1 - my_block) * lanes])
    starts = (begin[None, :] + jnp.array([0, split // 128])[:, None]).reshape(-1)
    return exchange(starts, sources, factors, gram, 3, [early, early_other, late, late_other], 2 * columns)


def many_blocks(coeff, intersection, basis_vals, factors, capacity, steps):
    num_clusters, list_len = intersection.shape
    atom_count, num_funcs, columns = coeff.shape
    my_cluster = lax.axis_index("cluster")
    num_blocks = lax.axis_size("blk")
    local_atom = intersection - my_cluster * atom_count
    mine = jnp.logical_and(local_atom >= 0, local_atom < atom_count)
    earlier = jnp.arange(list_len)[:, None] < jnp.arange(list_len)[None, :]
    rank = dot_nn(mine.astype(jnp.bfloat16), earlier.astype(jnp.bfloat16)).astype(jnp.int32)
    matches = jnp.logical_and(mine[:, None, :], rank[:, None, :] == jnp.arange(capacity)[None, :, None])
    source_rows = jnp.sum(jnp.where(matches, local_atom[:, None, :], 0), axis=2)
    outgoing = coeff.at[source_rows.reshape(-1)].get(mode="promise_in_bounds")
    outgoing = outgoing.reshape(num_clusters, capacity, num_funcs, columns)
    incoming = lax.all_to_all(outgoing, "cluster", split_axis=0, concat_axis=0, tiled=True)
    my_row = lax.dynamic_index_in_dim(intersection, my_cluster, 0, keepdims=False)
    my_owners = my_row // atom_count
    same = jnp.logical_and(my_owners[:, None] == my_owners[None, :], earlier.T)
    positions = my_owners * capacity + jnp.sum(same.astype(jnp.int32), axis=1)
    needed = incoming.reshape(num_clusters * capacity, num_funcs, columns)
    needed = needed.at[positions].get(mode="promise_in_bounds")
    needed = needed.reshape(list_len * num_funcs, columns)
    all_columns = lax.all_gather(needed, "blk", axis=1, tiled=True)
    sources = [basis_vals if step == 0 else passed_along(basis_vals, "blk", -step) for step in steps]
    starts = jnp.zeros((1,), jnp.int32)
    return exchange(starts, sources, factors, None, 0, [all_columns], num_blocks * columns)


def on_device(coeff, intersection, basis_vals, coulomb, reach):
    num_clusters = lax.axis_size("cluster")
    num_blocks = lax.axis_size("blk")
    list_len = intersection.shape[1]
    capacity = 2 * list_len // num_clusters
    half_stops = (coulomb.shape[1] - 1) // 2
    by_step = {}
    for offset in range(-half_stops, half_stops + 1):
        by_step.setdefault(offset % num_blocks, []).append(offset)
    factors = screened_factors(coulomb, reach, by_step, (coeff.shape[2] * num_blocks) ** (-0.5))
    if takes_two_blocks(num_clusters, num_blocks):
        return two_blocks(coeff, intersection, basis_vals, factors, capacity)
    return many_blocks(coeff, intersection, basis_vals, factors, capacity, sorted(by_step))


def takes_two_blocks(num_clusters, num_blocks):
    return num_blocks == 2 and num_clusters >= 16 and num_clusters & (num_clusters - 1) == 0


def solution(mesh):
    return jax.shard_map(
        on_device,
        mesh=mesh,
        in_specs=(
            P("cluster", None, "blk"),
            P(),
            P(("cluster", "blk"), None),
            P(("cluster", "blk"), None, None),
            P(("cluster", "blk")),
        ),
        out_specs=P(("cluster", "blk"), None),
        check_vma=False,
    )
```

```python
import jax
import jax.numpy as jnp
from jax import lax
from jax.experimental import pallas as pl
from jax.experimental.pallas import tpu as pltpu
from jax.sharding import PartitionSpec as P


EARLY_PARTS = 5

VMEM = pl.BlockSpec(memory_space=pltpu.VMEM)
SMEM = pl.BlockSpec(memory_space=pltpu.SMEM)
HBM = pl.BlockSpec(memory_space=pltpu.HBM)
PARAMS = pltpu.CompilerParams(vmem_limit_bytes=12 * 2**20)


def passed_along(value, axis, steps):
    count = lax.axis_size(axis)
    pairs = [(source, (source + steps) % count) for source in range(count)]
    return lax.ppermute(value, axis, pairs)


def swapped(value, axis, bits):
    count = lax.axis_size(axis)
    return lax.ppermute(value, axis, [(source, source ^ bits) for source in range(count)])


def dot_nn(a, b):
    return lax.dot_general(a, b, (((1,), (0,)), ((), ())), preferred_element_type=jnp.float32)


def dot_nt(a, b):
    return lax.dot_general(a, b, (((1,), (1,)), ((), ())), preferred_element_type=jnp.float32)


def orbital_block(basis_refs, values):
    return jnp.concatenate([dot_nn(ref[...], values).astype(jnp.bfloat16) for ref in basis_refs], axis=0)


def orbitals_of(sources, values, density=None):
    num_sources = len(sources)
    points = sources[0].shape[0]

    def kernel(*refs):
        orbitals = orbital_block(refs[:num_sources], refs[num_sources][...])
        orbital_ref, density_ref = refs[-2:]
        orbital_ref[...] = orbitals
        total = dot_nt(orbitals[:points], orbitals)
        density_ref[...] = total if density is None else total + refs[num_sources + 1][...]

    operands = [*sources, values]
    if density is not None:
        operands.append(density)
    return pl.pallas_call(
        kernel,
        out_shape=[
            jax.ShapeDtypeStruct((num_sources * points, values.shape[1]), jnp.bfloat16),
            jax.ShapeDtypeStruct((points, num_sources * points), jnp.float32),
        ],
        in_specs=[VMEM] * len(operands),
        out_specs=[VMEM, VMEM],
        compiler_params=PARAMS,
        name="orbitals_of",
    )(*operands)


def exchange(starts, sources, factors, density, orbitals, values, width):
    num_sources = len(sources)
    num_known = len(orbitals)
    points = sources[0].shape[0]
    widths = [block.shape[1] for block in orbitals] + [values.shape[1]]

    def kernel(*refs):
        start_ref = refs[0]
        basis_refs = refs[1 : 1 + num_sources]
        factor_refs = refs[1 + num_sources : 1 + 2 * num_sources]
        rest = list(refs[1 + 2 * num_sources :])
        total = rest.pop(0)[...] if density is not None else None
        known_refs = rest[:num_known]
        value_ref, out_ref = rest[num_known : num_known + 2]
        held_refs = rest[num_known + 2 : -2]
        last_ref, sems = rest[-2:]
        last_ref[...] = orbital_block(basis_refs, value_ref[...])
        term = dot_nt(last_ref[:points], last_ref[...])
        total = term if total is None else total + term
        tiles = []
        for source in range(num_sources):
            part = total[:, source * points : (source + 1) * points]
            tiles.append((part * factor_refs[source][...]).astype(jnp.bfloat16))
        tiles = jnp.concatenate(tiles, axis=1)
        copies = []
        for at, ref in enumerate([*known_refs, last_ref]):
            held_refs[at][...] = dot_nn(tiles, ref[...]).astype(out_ref.dtype)
            start = pl.multiple_of(start_ref[at] * 128, 128)
            copy = pltpu.make_async_copy(held_refs[at], out_ref.at[:, pl.ds(start, widths[at])], sems.at[at])
            copy.start()
            copies.append(copy)
        for copy in copies:
            copy.wait()

    operands = [starts, *sources, *factors]
    if density is not None:
        operands.append(density)
    operands.extend([*orbitals, values])
    return pl.pallas_call(
        kernel,
        out_shape=jax.ShapeDtypeStruct((points, width), jnp.bfloat16),
        in_specs=[SMEM] + [VMEM] * (len(operands) - 1),
        out_specs=HBM,
        scratch_shapes=[pltpu.VMEM((points, columns), jnp.bfloat16) for columns in widths]
        + [pltpu.VMEM((num_sources * points, widths[-1]), jnp.bfloat16), pltpu.SemaphoreType.DMA((len(widths),))],
        compiler_params=PARAMS if num_sources == 2 else pltpu.CompilerParams(vmem_limit_bytes=32 * 2**20),
        name="exchange",
    )(*operands)


def second_halves(blocks):
    rows = blocks[0].shape[0]
    half = rows // 2

    def kernel(*refs):
        for at, ref in enumerate(refs[:-1]):
            refs[-1][at * half : (at + 1) * half] = ref[half:]

    return pl.pallas_call(
        kernel,
        out_shape=jax.ShapeDtypeStruct((len(blocks) * half,) + blocks[0].shape[1:], blocks[0].dtype),
        in_specs=[VMEM] * len(blocks),
        out_specs=VMEM,
        compiler_params=PARAMS,
        name="second_halves",
    )(*blocks)


def outgoing(coeff, intersection, my_cluster, capacity, split):
    num_clusters, list_len = intersection.shape
    atom_count, num_funcs, columns = coeff.shape
    slots = num_clusters * capacity
    lanes = 128

    def kernel(me_ref, list_ref, coeff_ref, list_held, late_ref, *rest):
        early_refs = rest[: num_clusters // 2]
        coeff_held, late_held, source_held, source_read, sems = rest[num_clusters // 2 :]
        coeff_copy = pltpu.make_async_copy(coeff_ref, coeff_held, sems.at[0])
        list_copy = pltpu.make_async_copy(list_ref, list_held, sems.at[1])
        late_copy = pltpu.make_async_copy(late_held, late_ref, sems.at[2])
        source_copy = pltpu.make_async_copy(source_held, source_read, sems.at[3])
        list_copy.start()
        coeff_copy.start()
        me = me_ref[0]
        ks = lax.broadcasted_iota(jnp.int32, (list_len, list_len), 0)
        ls = lax.broadcasted_iota(jnp.int32, (list_len, list_len), 1)
        earlier = jnp.where(ks < ls, 1.0, 0.0).astype(jnp.bfloat16)
        list_copy.wait()
        local = list_held[...] - me * atom_count
        mine = jnp.logical_and(local >= 0, local < atom_count)
        rank = dot_nn(jnp.where(mine, 1.0, 0.0).astype(jnp.bfloat16), earlier)
        lane = lax.broadcasted_iota(jnp.int32, (num_clusters, lanes), 1)
        source = jnp.zeros((num_clusters, lanes), jnp.int32)
        for slot in range(capacity):
            chosen = jnp.where(jnp.logical_and(mine, rank == slot), local, 0)
            source = jnp.where(lane == slot, jnp.sum(chosen, axis=1, keepdims=True), source)
        source_held[...] = source
        source_copy.start()
        source_copy.wait()
        coeff_copy.wait()
        for cluster in range(num_clusters):
            for slot in range(capacity):
                late_held[cluster * capacity + slot] = coeff_held[source_read[cluster, slot], :, split:]
        late_copy.start()
        for turn in range(num_clusters):
            cluster = jnp.bitwise_xor(me, turn)
            for slot in range(capacity):
                values = coeff_held[source_read[cluster, slot], :, :split]
                early_refs[turn // 2][turn % 2 * capacity + slot] = values
        late_copy.wait()

    count = num_clusters // 2
    late = jax.ShapeDtypeStruct((slots, num_funcs, columns - split), coeff.dtype)
    early = jax.ShapeDtypeStruct((2 * capacity, num_funcs, split), coeff.dtype)
    return pl.pallas_call(
        kernel,
        out_shape=[jax.ShapeDtypeStruct(intersection.shape, jnp.int32), late] + [early] * count,
        in_specs=[SMEM, HBM, HBM],
        out_specs=[VMEM, HBM] + [VMEM] * count,
        scratch_shapes=[
            pltpu.VMEM(coeff.shape, coeff.dtype),
            pltpu.VMEM((slots, num_funcs, columns - split), coeff.dtype),
            pltpu.VMEM((num_clusters, lanes), jnp.int32),
            pltpu.SMEM((num_clusters, lanes), jnp.int32),
            pltpu.SemaphoreType.DMA((4,)),
        ],
        compiler_params=PARAMS,
        name="outgoing",
    )(
        my_cluster.reshape(1),
        pltpu.with_memory_space_constraint(intersection, pltpu.HBM),
        pltpu.with_memory_space_constraint(coeff, pltpu.HBM),
    )


def packed(positions, blocks, taken, last):
    list_len = positions.shape[0]
    num_funcs, columns = last.shape[1:]
    slots = len(blocks) * taken + last.shape[0]

    def kernel(position_ref, *rest):
        last_ref, out_ref, held_ref = rest[len(blocks) :]
        for at, ref in enumerate(rest[: len(blocks)]):
            held_ref[at * taken : (at + 1) * taken] = ref[:taken]
        held_ref[len(blocks) * taken :] = last_ref[...]
        for k in range(list_len):
            out_ref[k] = held_ref[position_ref[k]]

    return pl.pallas_call(
        kernel,
        out_shape=jax.ShapeDtypeStruct((list_len, num_funcs, columns), last.dtype),
        in_specs=[SMEM] + [VMEM] * (len(blocks) + 1),
        out_specs=VMEM,
        scratch_shapes=[pltpu.VMEM((slots, num_funcs, columns), last.dtype)],
        compiler_params=PARAMS,
        name="packed",
    )(positions, *blocks, last).reshape(list_len * num_funcs, columns)


def screened_factors(coulomb, reach, by_step, norm_factor):
    half_stops = (coulomb.shape[1] - 1) // 2
    points = coulomb.shape[0]
    my_reach = reach[0]
    factors = []
    for step in sorted(by_step):
        total = jnp.zeros((points, coulomb.shape[2]), jnp.float32)
        for offset in by_step[step]:
            tile = coulomb[:, offset + half_stops, :].astype(jnp.float32)
            total = total + jnp.where(abs(offset) <= my_reach, tile, jnp.float32(0.0))
        factors.append(total * norm_factor)
    return factors


def two_blocks(coeff, intersection, basis_vals, factors, capacity):
    num_clusters, list_len = intersection.shape
    atom_count, num_funcs, columns = coeff.shape
    my_cluster = lax.axis_index("cluster")
    my_block = lax.axis_index("blk")
    split = max(columns * EARLY_PARTS // 8 // 128, 1) * 128
    listed, late, *pieces = outgoing(coeff, intersection, my_cluster, capacity, split)
    arrived = [pieces[0]]
    for m in range(1, len(pieces)):
        arrived.append(swapped(pieces[m], "cluster", 2 * m))
    late = late.reshape(num_clusters, capacity, num_funcs, columns - split)
    late = lax.all_to_all(late, "cluster", split_axis=0, concat_axis=0, tiled=True)
    late = late.reshape(num_clusters * capacity, num_funcs, columns - split)
    relayed = swapped(second_halves(arrived), "cluster", 1)
    sources = [basis_vals, swapped(basis_vals, "blk", 1)]

    my_row = lax.dynamic_index_in_dim(listed, my_cluster, 0, keepdims=False)
    owner = my_row // atom_count
    same = jnp.logical_and(owner[:, None] == owner[None, :], jnp.arange(list_len)[:, None] > jnp.arange(list_len)[None, :])
    rank = jnp.sum(same.astype(jnp.int32), axis=1)
    turn = jnp.bitwise_xor(owner, my_cluster)
    early_at = turn // 2 * capacity + rank + jnp.where(turn % 2 == 1, num_clusters // 2 * capacity, 0)
    late_at = owner * capacity + rank

    func = jnp.arange(list_len * num_funcs) % num_funcs
    late_row = jnp.repeat(late_at * num_funcs, num_funcs) + func
    late_order = late_row[:, None] == jnp.arange(num_clusters * capacity * num_funcs)[None, :]
    late_order = lax.optimization_barrier(late_order.astype(jnp.bfloat16))

    early = packed(early_at, arrived, capacity, relayed)
    early_other = swapped(early, "blk", 1)
    early_orbitals, density = orbitals_of(sources, early)
    late = dot_nn(late_order, late.reshape(-1, columns - split)).astype(jnp.bfloat16)
    late_other = swapped(late, "blk", 1)
    late_orbitals, density = orbitals_of(sources, late, density)
    early_other_orbitals, density = orbitals_of(sources, early_other, density)
    lanes = columns // 128
    begin = jnp.stack([my_block * lanes, (1 - my_block) * lanes])
    starts = (begin[None, :] + jnp.array([0, split // 128])[:, None]).reshape(-1)
    known = [early_orbitals, early_other_orbitals, late_orbitals]
    return exchange(starts, sources, factors, density, known, late_other, 2 * columns)


def many_blocks(coeff, intersection, basis_vals, factors, capacity, steps):
    num_clusters, list_len = intersection.shape
    atom_count, num_funcs, columns = coeff.shape
    my_cluster = lax.axis_index("cluster")
    num_blocks = lax.axis_size("blk")
    local_atom = intersection - my_cluster * atom_count
    mine = jnp.logical_and(local_atom >= 0, local_atom < atom_count)
    earlier = jnp.arange(list_len)[:, None] < jnp.arange(list_len)[None, :]
    rank = dot_nn(mine.astype(jnp.bfloat16), earlier.astype(jnp.bfloat16)).astype(jnp.int32)
    matches = jnp.logical_and(mine[:, None, :], rank[:, None, :] == jnp.arange(capacity)[None, :, None])
    source_rows = jnp.sum(jnp.where(matches, local_atom[:, None, :], 0), axis=2)
    outgoing = coeff.at[source_rows.reshape(-1)].get(mode="promise_in_bounds")
    outgoing = outgoing.reshape(num_clusters, capacity, num_funcs, columns)
    incoming = lax.all_to_all(outgoing, "cluster", split_axis=0, concat_axis=0, tiled=True)
    my_row = lax.dynamic_index_in_dim(intersection, my_cluster, 0, keepdims=False)
    my_owners = my_row // atom_count
    same = jnp.logical_and(my_owners[:, None] == my_owners[None, :], earlier.T)
    positions = my_owners * capacity + jnp.sum(same.astype(jnp.int32), axis=1)
    needed = incoming.reshape(num_clusters * capacity, num_funcs, columns)
    needed = needed.at[positions].get(mode="promise_in_bounds")
    needed = needed.reshape(list_len * num_funcs, columns)
    all_columns = lax.all_gather(needed, "blk", axis=1, tiled=True)
    sources = [basis_vals if step == 0 else passed_along(basis_vals, "blk", -step) for step in steps]
    starts = jnp.zeros((1,), jnp.int32)
    return exchange(starts, sources, factors, None, [], all_columns, num_blocks * columns)


def on_device(coeff, intersection, basis_vals, coulomb, reach):
    num_clusters = lax.axis_size("cluster")
    num_blocks = lax.axis_size("blk")
    list_len = intersection.shape[1]
    capacity = 2 * list_len // num_clusters
    half_stops = (coulomb.shape[1] - 1) // 2
    by_step = {}
    for offset in range(-half_stops, half_stops + 1):
        by_step.setdefault(offset % num_blocks, []).append(offset)
    factors = screened_factors(coulomb, reach, by_step, (coeff.shape[2] * num_blocks) ** (-0.5))
    if takes_two_blocks(num_clusters, num_blocks):
        return two_blocks(coeff, intersection, basis_vals, factors, capacity)
    return many_blocks(coeff, intersection, basis_vals, factors, capacity, sorted(by_step))


def takes_two_blocks(num_clusters, num_blocks):
    return num_blocks == 2 and num_clusters >= 16 and num_clusters & (num_clusters - 1) == 0


def solution(mesh):
    return jax.shard_map(
        on_device,
        mesh=mesh,
        in_specs=(
            P("cluster", None, "blk"),
            P(),
            P(("cluster", "blk"), None),
            P(("cluster", "blk"), None, None),
            P(("cluster", "blk")),
        ),
        out_specs=P(("cluster", "blk"), None),
        check_vma=False,
    )
```

```python
import jax
import jax.numpy as jnp
from jax import lax
from jax.experimental import pallas as pl
from jax.experimental.pallas import tpu as pltpu
from jax.sharding import PartitionSpec as P


EARLY_PARTS = 5

VMEM = pl.BlockSpec(memory_space=pltpu.VMEM)
SMEM = pl.BlockSpec(memory_space=pltpu.SMEM)
HBM = pl.BlockSpec(memory_space=pltpu.HBM)
PARAMS = pltpu.CompilerParams(vmem_limit_bytes=12 * 2**20)


def passed_along(value, axis, steps):
    count = lax.axis_size(axis)
    pairs = [(source, (source + steps) % count) for source in range(count)]
    return lax.ppermute(value, axis, pairs)


def swapped(value, axis, bits):
    count = lax.axis_size(axis)
    return lax.ppermute(value, axis, [(source, source ^ bits) for source in range(count)])


def dot_nn(a, b):
    return lax.dot_general(a, b, (((1,), (0,)), ((), ())), preferred_element_type=jnp.float32)


def dot_nt(a, b):
    return lax.dot_general(a, b, (((1,), (1,)), ((), ())), preferred_element_type=jnp.float32)


def orbital_block(basis_refs, values):
    return jnp.concatenate([dot_nn(ref[...], values).astype(jnp.bfloat16) for ref in basis_refs], axis=0)


def orbitals_of(sources, values, density=None):
    num_sources = len(sources)
    points = sources[0].shape[0]

    def kernel(*refs):
        orbitals = orbital_block(refs[:num_sources], refs[num_sources][...])
        orbital_ref, density_ref = refs[-2:]
        orbital_ref[...] = orbitals
        total = dot_nt(orbitals[:points], orbitals)
        density_ref[...] = total if density is None else total + refs[num_sources + 1][...]

    operands = [*sources, values]
    if density is not None:
        operands.append(density)
    return pl.pallas_call(
        kernel,
        out_shape=[
            jax.ShapeDtypeStruct((num_sources * points, values.shape[1]), jnp.bfloat16),
            jax.ShapeDtypeStruct((points, num_sources * points), jnp.float32),
        ],
        in_specs=[VMEM] * len(operands),
        out_specs=[VMEM, VMEM],
        compiler_params=PARAMS,
        name="orbitals_of",
    )(*operands)


def exchange(places, sources, factors, density, orbitals, values, width):
    num_sources = len(sources)
    num_known = len(orbitals)
    points = sources[0].shape[0]
    widths = [block.shape[1] for block in orbitals] + [values.shape[1]]

    num_blocks = lax.axis_size("blk")

    def kernel(*refs):
        basis_refs = refs[:num_sources]
        factor_refs = refs[num_sources : 2 * num_sources]
        rest = list(refs[2 * num_sources :])
        my_block = lax.axis_index("blk")
        total = rest.pop(0)[...] if density is not None else None
        known_refs = rest[:num_known]
        value_ref, out_ref = rest[num_known : num_known + 2]
        held_refs = rest[num_known + 2 : -2]
        last_ref, sems = rest[-2:]
        last_ref[...] = orbital_block(basis_refs, value_ref[...])
        term = dot_nt(last_ref[:points], last_ref[...])
        total = term if total is None else total + term
        tiles = []
        for source in range(num_sources):
            part = total[:, source * points : (source + 1) * points]
            tiles.append((part * factor_refs[source][...]).astype(jnp.bfloat16))
        tiles = jnp.concatenate(tiles, axis=1)
        copies = []
        for at, ref in enumerate([*known_refs, last_ref]):
            held_refs[at][...] = dot_nn(tiles, ref[...]).astype(out_ref.dtype)
            turn, first = places[at]
            start = lax.rem(my_block + turn, num_blocks) * (width // num_blocks) + first if turn is not None else first
            start = pl.multiple_of(start, 128)
            copy = pltpu.make_async_copy(held_refs[at], out_ref.at[:, pl.ds(start, widths[at])], sems.at[at])
            copy.start()
            copies.append(copy)
        for copy in copies:
            copy.wait()

    operands = [*sources, *factors]
    if density is not None:
        operands.append(density)
    operands.extend([*orbitals, values])
    return pl.pallas_call(
        kernel,
        out_shape=jax.ShapeDtypeStruct((points, width), jnp.bfloat16),
        in_specs=[VMEM] * len(operands),
        out_specs=HBM,
        scratch_shapes=[pltpu.VMEM((points, columns), jnp.bfloat16) for columns in widths]
        + [pltpu.VMEM((num_sources * points, widths[-1]), jnp.bfloat16), pltpu.SemaphoreType.DMA((len(widths),))],
        compiler_params=PARAMS if num_sources == 2 else pltpu.CompilerParams(vmem_limit_bytes=32 * 2**20),
        name="exchange",
    )(*operands)


def second_halves(blocks):
    rows = blocks[0].shape[0]
    half = rows // 2

    def kernel(*refs):
        for at, ref in enumerate(refs[:-1]):
            refs[-1][at * half : (at + 1) * half] = ref[half:]

    return pl.pallas_call(
        kernel,
        out_shape=jax.ShapeDtypeStruct((len(blocks) * half,) + blocks[0].shape[1:], blocks[0].dtype),
        in_specs=[VMEM] * len(blocks),
        out_specs=VMEM,
        compiler_params=PARAMS,
        name="second_halves",
    )(*blocks)


def outgoing(coeff, intersection, basis_vals, capacity, split):
    num_clusters, list_len = intersection.shape
    atom_count, num_funcs, columns = coeff.shape
    slots = num_clusters * capacity
    lanes = 128

    def kernel(list_ref, coeff_ref, basis_ref, early_at_ref, late_at_ref, basis_held, late_ref, *rest):
        early_refs = rest[: num_clusters // 2]
        list_held, coeff_held, late_held, source_held, source_read, sems = rest[num_clusters // 2 :]
        coeff_copy = pltpu.make_async_copy(coeff_ref, coeff_held, sems.at[0])
        list_copy = pltpu.make_async_copy(list_ref, list_held, sems.at[1])
        late_copy = pltpu.make_async_copy(late_held, late_ref, sems.at[2])
        source_copy = pltpu.make_async_copy(source_held, source_read, sems.at[3])
        basis_copy = pltpu.make_async_copy(basis_ref, basis_held, sems.at[4])
        list_copy.start()
        coeff_copy.start()
        basis_copy.start()
        me = lax.axis_index("cluster")
        ks = lax.broadcasted_iota(jnp.int32, (list_len, list_len), 0)
        ls = lax.broadcasted_iota(jnp.int32, (list_len, list_len), 1)
        earlier = jnp.where(ks < ls, 1.0, 0.0).astype(jnp.bfloat16)
        list_copy.wait()
        local = list_held[...] - me * atom_count
        mine = jnp.logical_and(local >= 0, local < atom_count)
        rank = dot_nn(jnp.where(mine, 1.0, 0.0).astype(jnp.bfloat16), earlier)
        lane = lax.broadcasted_iota(jnp.int32, (num_clusters, lanes), 1)
        source = jnp.zeros((num_clusters, lanes), jnp.int32)
        for slot in range(capacity):
            chosen = jnp.where(jnp.logical_and(mine, rank == slot), local, 0)
            source = jnp.where(lane == slot, jnp.sum(chosen, axis=1, keepdims=True), source)
        source_held[...] = source
        source_copy.start()
        owner = jnp.broadcast_to(list_held[pl.ds(me, 1)], (list_len, list_len)) // atom_count
        owner_across = jnp.sum(jnp.where(ks == ls, owner, 0), axis=1, keepdims=True)
        before = jnp.where(jnp.logical_and(owner == owner_across, ks < ls), 1, 0)
        slot = jnp.sum(before, axis=0, keepdims=True)
        owner = owner[:1]
        turn = jnp.bitwise_xor(owner, me)
        side = jnp.bitwise_and(turn, 1)
        early_at_ref[...] = (turn - side) // 2 * capacity + side * (slots // 2) + slot
        late_at_ref[...] = owner * capacity + slot
        source_copy.wait()
        coeff_copy.wait()
        for cluster in range(num_clusters):
            for slot in range(capacity):
                late_held[cluster * capacity + slot] = coeff_held[source_read[cluster, slot], :, split:]
        late_copy.start()
        for turn in range(num_clusters):
            cluster = jnp.bitwise_xor(me, turn)
            for slot in range(capacity):
                values = coeff_held[source_read[cluster, slot], :, :split]
                early_refs[turn // 2][turn % 2 * capacity + slot] = values
        late_copy.wait()
        basis_copy.wait()

    count = num_clusters // 2
    late = jax.ShapeDtypeStruct((slots, num_funcs, columns - split), coeff.dtype)
    early = jax.ShapeDtypeStruct((2 * capacity, num_funcs, split), coeff.dtype)
    return pl.pallas_call(
        kernel,
        out_shape=[
            jax.ShapeDtypeStruct((1, list_len), jnp.int32),
            jax.ShapeDtypeStruct((1, list_len), jnp.int32),
            jax.ShapeDtypeStruct(basis_vals.shape, basis_vals.dtype),
            late,
        ]
        + [early] * count,
        in_specs=[HBM] * 3,
        out_specs=[VMEM, VMEM, VMEM, HBM] + [VMEM] * count,
        scratch_shapes=[
            pltpu.VMEM(intersection.shape, jnp.int32),
            pltpu.VMEM(coeff.shape, coeff.dtype),
            pltpu.VMEM((slots, num_funcs, columns - split), coeff.dtype),
            pltpu.VMEM((num_clusters, lanes), jnp.int32),
            pltpu.SMEM((num_clusters, lanes), jnp.int32),
            pltpu.SemaphoreType.DMA((5,)),
        ],
        compiler_params=PARAMS,
        name="outgoing",
    )(
        pltpu.with_memory_space_constraint(intersection, pltpu.HBM),
        pltpu.with_memory_space_constraint(coeff, pltpu.HBM),
        pltpu.with_memory_space_constraint(basis_vals, pltpu.HBM),
    )


def packed(positions, blocks, taken, last):
    list_len = positions.shape[1]
    num_funcs, columns = last.shape[1:]
    slots = len(blocks) * taken + last.shape[0]

    def kernel(position_ref, *rest):
        last_ref, out_ref, held_ref = rest[len(blocks) :]
        for at, ref in enumerate(rest[: len(blocks)]):
            held_ref[at * taken : (at + 1) * taken] = ref[:taken]
        held_ref[len(blocks) * taken :] = last_ref[...]
        for k in range(list_len):
            out_ref[k] = held_ref[position_ref[0, k]]

    return pl.pallas_call(
        kernel,
        out_shape=jax.ShapeDtypeStruct((list_len, num_funcs, columns), last.dtype),
        in_specs=[SMEM] + [VMEM] * (len(blocks) + 1),
        out_specs=VMEM,
        scratch_shapes=[pltpu.VMEM((slots, num_funcs, columns), last.dtype)],
        compiler_params=PARAMS,
        name="packed",
    )(positions, *blocks, last).reshape(list_len * num_funcs, columns)


def screened_factors(coulomb, reach, by_step, norm_factor):
    half_stops = (coulomb.shape[1] - 1) // 2
    points = coulomb.shape[0]
    my_reach = reach[0]
    factors = []
    for step in sorted(by_step):
        total = jnp.zeros((points, coulomb.shape[2]), jnp.float32)
        for offset in by_step[step]:
            tile = coulomb[:, offset + half_stops, :].astype(jnp.float32)
            total = total + jnp.where(abs(offset) <= my_reach, tile, jnp.float32(0.0))
        factors.append(total * norm_factor)
    return factors


def two_blocks(coeff, intersection, basis_vals, factors, capacity):
    num_clusters, list_len = intersection.shape
    _, num_funcs, columns = coeff.shape
    split = max(columns * EARLY_PARTS // 8 // 128, 1) * 128
    early_at, late_at, basis, late, *pieces = outgoing(coeff, intersection, basis_vals, capacity, split)
    arrived = [pieces[0]]
    for m in range(1, len(pieces)):
        arrived.append(swapped(pieces[m], "cluster", 2 * m))
    late = late.reshape(num_clusters, capacity, num_funcs, columns - split)
    late = lax.all_to_all(late, "cluster", split_axis=0, concat_axis=0, tiled=True)
    late = late.reshape(num_clusters * capacity, num_funcs, columns - split)
    relayed = swapped(second_halves(arrived), "cluster", 1)
    sources = [basis, swapped(basis, "blk", 1)]

    func = jnp.arange(list_len * num_funcs) % num_funcs
    late_row = jnp.repeat(late_at.reshape(-1) * num_funcs, num_funcs) + func
    late_row = lax.optimization_barrier(late_row)
    late_order = late_row[:, None] == jnp.arange(num_clusters * capacity * num_funcs)[None, :]
    late_order = lax.optimization_barrier(late_order.astype(jnp.bfloat16))

    early = packed(early_at, arrived, capacity, relayed)
    early_other = swapped(early, "blk", 1)
    early_orbitals, density = orbitals_of(sources, early)
    late = dot_nn(late_order, late.reshape(-1, columns - split)).astype(jnp.bfloat16)
    late_other = swapped(late, "blk", 1)
    late_orbitals, density = orbitals_of(sources, late, density)
    early_other_orbitals, density = orbitals_of(sources, early_other, density)
    places = [(0, 0), (1, 0), (0, split), (1, split)]
    known = [early_orbitals, early_other_orbitals, late_orbitals]
    return exchange(places, sources, factors, density, known, late_other, 2 * columns)


def many_blocks(coeff, intersection, basis_vals, factors, capacity, steps):
    num_clusters, list_len = intersection.shape
    atom_count, num_funcs, columns = coeff.shape
    my_cluster = lax.axis_index("cluster")
    num_blocks = lax.axis_size("blk")
    local_atom = intersection - my_cluster * atom_count
    mine = jnp.logical_and(local_atom >= 0, local_atom < atom_count)
    earlier = jnp.arange(list_len)[:, None] < jnp.arange(list_len)[None, :]
    rank = dot_nn(mine.astype(jnp.bfloat16), earlier.astype(jnp.bfloat16)).astype(jnp.int32)
    matches = jnp.logical_and(mine[:, None, :], rank[:, None, :] == jnp.arange(capacity)[None, :, None])
    source_rows = jnp.sum(jnp.where(matches, local_atom[:, None, :], 0), axis=2)
    outgoing = coeff.at[source_rows.reshape(-1)].get(mode="promise_in_bounds")
    outgoing = outgoing.reshape(num_clusters, capacity, num_funcs, columns)
    incoming = lax.all_to_all(outgoing, "cluster", split_axis=0, concat_axis=0, tiled=True)
    my_row = lax.dynamic_index_in_dim(intersection, my_cluster, 0, keepdims=False)
    my_owners = my_row // atom_count
    same = jnp.logical_and(my_owners[:, None] == my_owners[None, :], earlier.T)
    positions = my_owners * capacity + jnp.sum(same.astype(jnp.int32), axis=1)
    needed = incoming.reshape(num_clusters * capacity, num_funcs, columns)
    needed = needed.at[positions].get(mode="promise_in_bounds")
    needed = needed.reshape(list_len * num_funcs, columns)
    all_columns = lax.all_gather(needed, "blk", axis=1, tiled=True)
    sources = [basis_vals if step == 0 else passed_along(basis_vals, "blk", -step) for step in steps]
    return exchange([(None, 0)], sources, factors, None, [], all_columns, num_blocks * columns)


def on_device(coeff, intersection, basis_vals, coulomb, reach):
    num_clusters = lax.axis_size("cluster")
    num_blocks = lax.axis_size("blk")
    list_len = intersection.shape[1]
    capacity = 2 * list_len // num_clusters
    half_stops = (coulomb.shape[1] - 1) // 2
    by_step = {}
    for offset in range(-half_stops, half_stops + 1):
        by_step.setdefault(offset % num_blocks, []).append(offset)
    factors = screened_factors(coulomb, reach, by_step, (coeff.shape[2] * num_blocks) ** (-0.5))
    if takes_two_blocks(num_clusters, num_blocks):
        return two_blocks(coeff, intersection, basis_vals, factors, capacity)
    return many_blocks(coeff, intersection, basis_vals, factors, capacity, sorted(by_step))


def takes_two_blocks(num_clusters, num_blocks):
    return num_blocks == 2 and num_clusters >= 16 and num_clusters & (num_clusters - 1) == 0


def solution(mesh):
    return jax.shard_map(
        on_device,
        mesh=mesh,
        in_specs=(
            P("cluster", None, "blk"),
            P(),
            P(("cluster", "blk"), None),
            P(("cluster", "blk"), None, None),
            P(("cluster", "blk")),
        ),
        out_specs=P(("cluster", "blk"), None),
        check_vma=False,
    )
```

```python
import jax
import jax.numpy as jnp
from jax import lax
from jax.experimental import pallas as pl
from jax.experimental.pallas import tpu as pltpu
from jax.sharding import PartitionSpec as P


EARLY_PARTS = 5

VMEM = pl.BlockSpec(memory_space=pltpu.VMEM)
SMEM = pl.BlockSpec(memory_space=pltpu.SMEM)
HBM = pl.BlockSpec(memory_space=pltpu.HBM)
PARAMS = pltpu.CompilerParams(vmem_limit_bytes=12 * 2**20)


def passed_along(value, axis, steps):
    count = lax.axis_size(axis)
    pairs = [(source, (source + steps) % count) for source in range(count)]
    return lax.ppermute(value, axis, pairs)


def swapped(value, axis, bits):
    count = lax.axis_size(axis)
    return lax.ppermute(value, axis, [(source, source ^ bits) for source in range(count)])


def dot_nn(a, b):
    return lax.dot_general(a, b, (((1,), (0,)), ((), ())), preferred_element_type=jnp.float32)


def dot_nt(a, b):
    return lax.dot_general(a, b, (((1,), (1,)), ((), ())), preferred_element_type=jnp.float32)


def orbital_block(basis_refs, values):
    return jnp.concatenate([dot_nn(ref[...], values).astype(jnp.bfloat16) for ref in basis_refs], axis=0)


def orbitals_of(sources, values, density=None):
    num_sources = len(sources)
    points = sources[0].shape[0]

    def kernel(*refs):
        orbitals = orbital_block(refs[:num_sources], refs[num_sources][...])
        orbital_ref, density_ref = refs[-2:]
        orbital_ref[...] = orbitals
        total = dot_nt(orbitals[:points], orbitals)
        density_ref[...] = total if density is None else total + refs[num_sources + 1][...]

    operands = [*sources, values]
    if density is not None:
        operands.append(density)
    return pl.pallas_call(
        kernel,
        out_shape=[
            jax.ShapeDtypeStruct((num_sources * points, values.shape[1]), jnp.bfloat16),
            jax.ShapeDtypeStruct((points, num_sources * points), jnp.float32),
        ],
        in_specs=[VMEM] * len(operands),
        out_specs=[VMEM, VMEM],
        compiler_params=PARAMS,
        name="orbitals_of",
    )(*operands)


def exchange(sides, sources, factors, density, orbitals, values, width):
    num_sources = len(sources)
    num_known = len(orbitals)
    points = sources[0].shape[0]
    side_width = width // len(sides)
    step = side_width // 2 if side_width % 512 == 0 else side_width
    num_pieces = width // step

    def kernel(*refs):
        basis_refs = refs[:num_sources]
        factor_refs = refs[num_sources : 2 * num_sources]
        rest = list(refs[2 * num_sources :])
        my_block = lax.axis_index("blk")
        total = rest.pop(0)[...] if density is not None else None
        known_refs = rest[:num_known]
        value_ref, out_ref = rest[num_known : num_known + 2]
        held_refs = rest[num_known + 2 : -2]
        last_ref, sems = rest[-2:]
        last_ref[...] = orbital_block(basis_refs, value_ref[...])
        term = dot_nt(last_ref[:points], last_ref[...])
        total = term if total is None else total + term
        tiles = []
        for source in range(num_sources):
            part = total[:, source * points : (source + 1) * points]
            tiles.append((part * factor_refs[source][...]).astype(jnp.bfloat16))
        tiles = jnp.concatenate(tiles, axis=1)
        copies = []
        all_refs = [*known_refs, last_ref]
        for turn, members in enumerate(sides):
            blocks = [all_refs[at] for at in members]
            for begin in range(0, side_width, step):
                at = turn * (side_width // step) + begin // step
                held_ref = held_refs[at]
                held_ref[...] = dot_nn(tiles, columns_of(blocks, begin, begin + step)).astype(out_ref.dtype)
                start = begin
                if len(sides) > 1:
                    start = lax.rem(my_block + turn, len(sides)) * side_width + begin
                start = pl.multiple_of(start, 128)
                copy = pltpu.make_async_copy(held_ref, out_ref.at[:, pl.ds(start, step)], sems.at[at])
                copy.start()
                copies.append(copy)
        for copy in copies:
            copy.wait()

    operands = [*sources, *factors]
    if density is not None:
        operands.append(density)
    operands.extend([*orbitals, values])
    return pl.pallas_call(
        kernel,
        out_shape=jax.ShapeDtypeStruct((points, width), jnp.bfloat16),
        in_specs=[VMEM] * len(operands),
        out_specs=HBM,
        scratch_shapes=[pltpu.VMEM((points, step), jnp.bfloat16)] * num_pieces
        + [pltpu.VMEM((num_sources * points, values.shape[1]), jnp.bfloat16), pltpu.SemaphoreType.DMA((num_pieces,))],
        compiler_params=pltpu.CompilerParams(vmem_limit_bytes=12 * 2**20) if num_sources == 2 else pltpu.CompilerParams(vmem_limit_bytes=32 * 2**20),
        name="exchange",
    )(*operands)


def columns_of(blocks, begin, end):
    found = []
    first = 0
    for block in blocks:
        width = block.shape[1]
        low, high = max(begin - first, 0), min(end - first, width)
        if low < high:
            found.append(block[:, low:high])
        first += width
    return found[0] if len(found) == 1 else jnp.concatenate(found, axis=1)


def second_halves(blocks):
    rows = blocks[0].shape[0]
    half = rows // 2

    def kernel(*refs):
        for at, ref in enumerate(refs[:-1]):
            refs[-1][at * half : (at + 1) * half] = ref[half:]

    return pl.pallas_call(
        kernel,
        out_shape=jax.ShapeDtypeStruct((len(blocks) * half,) + blocks[0].shape[1:], blocks[0].dtype),
        in_specs=[VMEM] * len(blocks),
        out_specs=VMEM,
        compiler_params=PARAMS,
        name="second_halves",
    )(*blocks)


def outgoing(coeff, intersection, basis_vals, capacity, split):
    num_clusters, list_len = intersection.shape
    atom_count, num_funcs, columns = coeff.shape
    slots = num_clusters * capacity
    lanes = 128

    def kernel(list_ref, coeff_ref, basis_ref, early_at_ref, late_at_ref, basis_held, late_ref, *rest):
        early_refs = rest[: num_clusters // 2]
        list_held, coeff_held, late_held, source_held, source_read, sems = rest[num_clusters // 2 :]
        coeff_copy = pltpu.make_async_copy(coeff_ref, coeff_held, sems.at[0])
        list_copy = pltpu.make_async_copy(list_ref, list_held, sems.at[1])
        late_copy = pltpu.make_async_copy(late_held, late_ref, sems.at[2])
        source_copy = pltpu.make_async_copy(source_held, source_read, sems.at[3])
        basis_copy = pltpu.make_async_copy(basis_ref, basis_held, sems.at[4])
        list_copy.start()
        coeff_copy.start()
        basis_copy.start()
        me = lax.axis_index("cluster")
        ks = lax.broadcasted_iota(jnp.int32, (list_len, list_len), 0)
        ls = lax.broadcasted_iota(jnp.int32, (list_len, list_len), 1)
        earlier = jnp.where(ks < ls, 1.0, 0.0).astype(jnp.bfloat16)
        list_copy.wait()
        local = list_held[...] - me * atom_count
        mine = jnp.logical_and(local >= 0, local < atom_count)
        rank = dot_nn(jnp.where(mine, 1.0, 0.0).astype(jnp.bfloat16), earlier)
        lane = lax.broadcasted_iota(jnp.int32, (num_clusters, lanes), 1)
        source = jnp.zeros((num_clusters, lanes), jnp.int32)
        for slot in range(capacity):
            chosen = jnp.where(jnp.logical_and(mine, rank == slot), local, 0)
            source = jnp.where(lane == slot, jnp.sum(chosen, axis=1, keepdims=True), source)
        source_held[...] = source
        source_copy.start()
        owner = jnp.broadcast_to(list_held[pl.ds(me, 1)], (list_len, list_len)) // atom_count
        owner_across = jnp.sum(jnp.where(ks == ls, owner, 0), axis=1, keepdims=True)
        before = jnp.where(jnp.logical_and(owner == owner_across, ks < ls), 1, 0)
        slot = jnp.sum(before, axis=0, keepdims=True)
        owner = owner[:1]
        turn = jnp.bitwise_xor(owner, me)
        side = jnp.bitwise_and(turn, 1)
        early_at_ref[...] = (turn - side) // 2 * capacity + side * (slots // 2) + slot
        late_at_ref[...] = owner * capacity + slot
        source_copy.wait()
        coeff_copy.wait()
        for cluster in range(num_clusters):
            for slot in range(capacity):
                late_held[cluster * capacity + slot] = coeff_held[source_read[cluster, slot], :, split:]
        late_copy.start()
        for turn in range(num_clusters):
            cluster = jnp.bitwise_xor(me, turn)
            for slot in range(capacity):
                values = coeff_held[source_read[cluster, slot], :, :split]
                early_refs[turn // 2][turn % 2 * capacity + slot] = values
        late_copy.wait()
        basis_copy.wait()

    count = num_clusters // 2
    late = jax.ShapeDtypeStruct((slots, num_funcs, columns - split), coeff.dtype)
    early = jax.ShapeDtypeStruct((2 * capacity, num_funcs, split), coeff.dtype)
    return pl.pallas_call(
        kernel,
        out_shape=[
            jax.ShapeDtypeStruct((1, list_len), jnp.int32),
            jax.ShapeDtypeStruct((1, list_len), jnp.int32),
            jax.ShapeDtypeStruct(basis_vals.shape, basis_vals.dtype),
            late,
        ]
        + [early] * count,
        in_specs=[HBM] * 3,
        out_specs=[VMEM, VMEM, VMEM, HBM] + [VMEM] * count,
        scratch_shapes=[
            pltpu.VMEM(intersection.shape, jnp.int32),
            pltpu.VMEM(coeff.shape, coeff.dtype),
            pltpu.VMEM((slots, num_funcs, columns - split), coeff.dtype),
            pltpu.VMEM((num_clusters, lanes), jnp.int32),
            pltpu.SMEM((num_clusters, lanes), jnp.int32),
            pltpu.SemaphoreType.DMA((5,)),
        ],
        compiler_params=PARAMS,
        name="outgoing",
    )(
        pltpu.with_memory_space_constraint(intersection, pltpu.HBM),
        pltpu.with_memory_space_constraint(coeff, pltpu.HBM),
        pltpu.with_memory_space_constraint(basis_vals, pltpu.HBM),
    )


def packed(positions, blocks, taken, last):
    list_len = positions.shape[1]
    num_funcs, columns = last.shape[1:]
    slots = len(blocks) * taken + last.shape[0]

    def kernel(position_ref, *rest):
        last_ref, out_ref, held_ref = rest[len(blocks) :]
        for at, ref in enumerate(rest[: len(blocks)]):
            held_ref[at * taken : (at + 1) * taken] = ref[:taken]
        held_ref[len(blocks) * taken :] = last_ref[...]
        for k in range(list_len):
            out_ref[k] = held_ref[position_ref[0, k]]

    return pl.pallas_call(
        kernel,
        out_shape=jax.ShapeDtypeStruct((list_len, num_funcs, columns), last.dtype),
        in_specs=[SMEM] + [VMEM] * (len(blocks) + 1),
        out_specs=VMEM,
        scratch_shapes=[pltpu.VMEM((slots, num_funcs, columns), last.dtype)],
        compiler_params=PARAMS,
        name="packed",
    )(positions, *blocks, last).reshape(list_len * num_funcs, columns)


def screened_factors(coulomb, reach, by_step, norm_factor):
    half_stops = (coulomb.shape[1] - 1) // 2
    points = coulomb.shape[0]
    my_reach = reach[0]
    factors = []
    for step in sorted(by_step):
        total = jnp.zeros((points, coulomb.shape[2]), jnp.float32)
        for offset in by_step[step]:
            tile = coulomb[:, offset + half_stops, :].astype(jnp.float32)
            total = total + jnp.where(abs(offset) <= my_reach, tile, jnp.float32(0.0))
        factors.append(total * norm_factor)
    return factors


def two_blocks(coeff, intersection, basis_vals, factors, capacity):
    num_clusters, list_len = intersection.shape
    _, num_funcs, columns = coeff.shape
    split = max(columns * EARLY_PARTS // 8 // 128, 1) * 128
    early_at, late_at, basis, late, *pieces = outgoing(coeff, intersection, basis_vals, capacity, split)
    arrived = [pieces[0]]
    for m in range(1, len(pieces)):
        arrived.append(swapped(pieces[m], "cluster", 2 * m))
    late = late.reshape(num_clusters, capacity, num_funcs, columns - split)
    late = lax.all_to_all(late, "cluster", split_axis=0, concat_axis=0, tiled=True)
    late = late.reshape(num_clusters * capacity, num_funcs, columns - split)
    relayed = swapped(second_halves(arrived), "cluster", 1)
    sources = [basis, swapped(basis, "blk", 1)]

    func = jnp.arange(list_len * num_funcs) % num_funcs
    late_row = jnp.repeat(late_at.reshape(-1) * num_funcs, num_funcs) + func
    late_row = lax.optimization_barrier(late_row)
    late_order = late_row[:, None] == jnp.arange(num_clusters * capacity * num_funcs)[None, :]
    late_order = lax.optimization_barrier(late_order.astype(jnp.bfloat16))

    early = packed(early_at, arrived, capacity, relayed)
    early_other = swapped(early, "blk", 1)
    early_orbitals, density = orbitals_of(sources, early)
    late = dot_nn(late_order, late.reshape(-1, columns - split)).astype(jnp.bfloat16)
    late_other = swapped(late, "blk", 1)
    late_orbitals, density = orbitals_of(sources, late, density)
    early_other_orbitals, density = orbitals_of(sources, early_other, density)
    known = [early_orbitals, early_other_orbitals, late_orbitals]
    return exchange([(0, 2), (1, 3)], sources, factors, density, known, late_other, 2 * columns)


def many_blocks(coeff, intersection, basis_vals, factors, capacity, steps):
    num_clusters, list_len = intersection.shape
    atom_count, num_funcs, columns = coeff.shape
    my_cluster = lax.axis_index("cluster")
    num_blocks = lax.axis_size("blk")
    local_atom = intersection - my_cluster * atom_count
    mine = jnp.logical_and(local_atom >= 0, local_atom < atom_count)
    earlier = jnp.arange(list_len)[:, None] < jnp.arange(list_len)[None, :]
    rank = dot_nn(mine.astype(jnp.bfloat16), earlier.astype(jnp.bfloat16)).astype(jnp.int32)
    matches = jnp.logical_and(mine[:, None, :], rank[:, None, :] == jnp.arange(capacity)[None, :, None])
    source_rows = jnp.sum(jnp.where(matches, local_atom[:, None, :], 0), axis=2)
    outgoing = coeff.at[source_rows.reshape(-1)].get(mode="promise_in_bounds")
    outgoing = outgoing.reshape(num_clusters, capacity, num_funcs, columns)
    incoming = lax.all_to_all(outgoing, "cluster", split_axis=0, concat_axis=0, tiled=True)
    my_row = lax.dynamic_index_in_dim(intersection, my_cluster, 0, keepdims=False)
    my_owners = my_row // atom_count
    same = jnp.logical_and(my_owners[:, None] == my_owners[None, :], earlier.T)
    positions = my_owners * capacity + jnp.sum(same.astype(jnp.int32), axis=1)
    needed = incoming.reshape(num_clusters * capacity, num_funcs, columns)
    needed = needed.at[positions].get(mode="promise_in_bounds")
    needed = needed.reshape(list_len * num_funcs, columns)
    all_columns = lax.all_gather(needed, "blk", axis=1, tiled=True)
    sources = [basis_vals if step == 0 else passed_along(basis_vals, "blk", -step) for step in steps]
    return exchange([(0,)], sources, factors, None, [], all_columns, num_blocks * columns)


def on_device(coeff, intersection, basis_vals, coulomb, reach):
    num_clusters = lax.axis_size("cluster")
    num_blocks = lax.axis_size("blk")
    list_len = intersection.shape[1]
    capacity = 2 * list_len // num_clusters
    half_stops = (coulomb.shape[1] - 1) // 2
    by_step = {}
    for offset in range(-half_stops, half_stops + 1):
        by_step.setdefault(offset % num_blocks, []).append(offset)
    factors = screened_factors(coulomb, reach, by_step, (coeff.shape[2] * num_blocks) ** (-0.5))
    if takes_two_blocks(num_clusters, num_blocks):
        return two_blocks(coeff, intersection, basis_vals, factors, capacity)
    return many_blocks(coeff, intersection, basis_vals, factors, capacity, sorted(by_step))


def takes_two_blocks(num_clusters, num_blocks):
    return num_blocks == 2 and num_clusters >= 16 and num_clusters & (num_clusters - 1) == 0


def solution(mesh):
    return jax.shard_map(
        on_device,
        mesh=mesh,
        in_specs=(
            P("cluster", None, "blk"),
            P(),
            P(("cluster", "blk"), None),
            P(("cluster", "blk"), None, None),
            P(("cluster", "blk")),
        ),
        out_specs=P(("cluster", "blk"), None),
        check_vma=False,
    )
```
